32 devices in a mesh: dp: 4 (over y, core), tm: 8 (over z, x).
Axes of the slice: x: 2, y: 2, z: 4, core: 2. Of those that a mesh axis runs over, the one named last changes fastest.
Arguments:
- features: bfloat16 [4, 8192, 512], P('dp', 'tm'), may hold values from -52 to 52
- conv_wide: bfloat16 [1536, 512], replicated, may hold values from -0.15625 to 0.15625
- conv_narrow: bfloat16 [1024, 512], replicated, may hold values from -0.1875 to 0.1875
- conv_bias: float32 [2, 512], replicated, may hold values from -4 to 4
- norm_gain: float32 [2, 512], replicated, may hold values from 0.1 to 1.9
- norm_bias: float32 [2, 512], replicated, may hold values from -3 to 3
- proj_gain: float32 [512], replicated, may hold values from 0.1 to 1.9
- proj_weight: bfloat16 [512, 1920], replicated, may hold values from -0.25 to 0.25
- proj_bias: float32 [1920], replicated, may hold values from -3 to 3
- upstream: bfloat16 [64, 2048, 120], P(('dp', 'tm')), may hold values from -6 to 6
Outputs:
- attn_input: bfloat16 [64, 2048, 120], P(('dp', 'tm'))
- feature_grad: bfloat16 [4, 8192, 512], P('dp', 'tm')
- grad_conv_wide: float32 [786432], P(('dp', 'tm'))
- grad_conv_narrow: float32 [524288], P(('dp', 'tm'))
The draws below stay inside these ranges and needn't reach their ends.
All inputs are finite; a program needn't handle non-finite values.
Results may differ from the reference program's by a relative error of at most 0.02.
Values may be sent and summed in bfloat16 or wider, within the bound.
No kernel may reach another device: no remote copies, remote signals or barrier semaphores. Data moves between devices by JAX's collectives and lax.ppermute only.
A program may use at most 128 MiB of HBM per device.

```python
import math
import jax
import jax.numpy as jnp
from jax import lax

CHANNELS = 512
WIDTH = 1920
HEADS = 16
HEAD_DIM = 120
LAYERS = 2
TAPS_WIDE = 3
TAPS_NARROW = 2
RECORDINGS = 4
TIME_ROWS = 8192
FRAMES = 2048


def draw_features(key, part):
    key_base, key_rough, key_chan = jax.random.split(key, 3)
    shape = (RECORDINGS, TIME_ROWS, CHANNELS)
    position = jnp.arange(TIME_ROWS, dtype=jnp.float32) / TIME_ROWS
    ramp = jnp.exp(jnp.log(3.0) * position)[None, :, None]
    rough = jnp.exp(jax.random.uniform(key_rough, (RECORDINGS, TIME_ROWS, 1), jnp.float32, -0.35, 0.35))
    channel_scale = jnp.exp(jax.random.uniform(key_chan, (1, 1, CHANNELS), jnp.float32, jnp.log(0.3), jnp.log(3.0)))
    base = jnp.clip(jax.random.normal(key_base, shape, jnp.float32), -4.0, 4.0)
    return (base * ramp * rough * channel_scale).astype(jnp.bfloat16)


def shard_levels(own_key, shape, shards, least, high):
    gain, own = 1.0, jax.random.fold_in(own_key, 6)
    for dim, blocks in shards:
        heights = jnp.exp(jax.random.uniform(jax.random.fold_in(own, dim), (blocks,), jnp.float32, least / len(shards), high / len(shards)))
        gain = gain * jnp.repeat(heights, shape[dim] // blocks).reshape([-1 if axis == dim else 1 for axis in range(len(shape))])
    return gain


def gaussian(key, dims, width, limit, cuts=(), kind=jnp.bfloat16):
    values = width * jax.random.normal(key, dims, jnp.float32)
    if cuts:
        values = values * shard_levels(key, dims, cuts, -0.22, 0.18)
    return jnp.clip(values, -limit, limit).astype(kind)


def setup_inputs(seed: int = 0) -> dict:
    arg_keys = jax.random.split(jax.random.key(seed), 11)
    return {
        "features": draw_features(jax.random.fold_in(arg_keys[10], 71), 0),
        "conv_wide": gaussian(arg_keys[1], (TAPS_WIDE * CHANNELS, CHANNELS), (TAPS_WIDE * CHANNELS) ** -0.5, 0.15625),
        "conv_narrow": gaussian(arg_keys[2], (TAPS_NARROW * CHANNELS, CHANNELS), (TAPS_NARROW * CHANNELS) ** -0.5, 0.1875),
        "conv_bias": gaussian(arg_keys[3], (LAYERS, CHANNELS), 1.0, 4.0, (), jnp.float32),
        "norm_gain": jnp.clip(1.0 + 0.18 * jax.random.normal(arg_keys[4], (LAYERS, CHANNELS), jnp.float32), 0.1, 1.9),
        "norm_bias": gaussian(arg_keys[5], (LAYERS, CHANNELS), 0.5, 3.0, (), jnp.float32),
        "proj_gain": jnp.clip(1.0 + 0.18 * jax.random.normal(arg_keys[6], (CHANNELS,), jnp.float32), 0.1, 1.9),
        "proj_weight": gaussian(arg_keys[7], (CHANNELS, WIDTH), CHANNELS ** -0.5, 0.25),
        "proj_bias": gaussian(arg_keys[8], (WIDTH,), 0.5, 3.0, (), jnp.float32),
        "upstream": gaussian(arg_keys[9], (RECORDINGS * HEADS, FRAMES, HEAD_DIM), 1.0, 6.0, ((0, 32),)),
    }


EPSILON = 1e-05
SQRT_HALF = 0.7071067811865476
INV_ROOT_TAU = 0.3989422804014327

def gelu_exact(values):
    return 0.5 * values * (1.0 + lax.erf(values * SQRT_HALF))

def gelu_slope(values):
    cumulative = 0.5 * (1.0 + lax.erf(values * SQRT_HALF))
    density = jnp.exp(-0.5 * values * values) * INV_ROOT_TAU
    return cumulative + values * density

def make_patches(signal, kernel_taps):
    length, channels_in = signal.shape
    paired = signal.reshape(length // 2, 2 * channels_in)
    if kernel_taps == 3:
        following = jnp.concatenate([paired[1:, :channels_in], jnp.zeros((1, channels_in), signal.dtype)], axis=0)
        return jnp.concatenate([paired, following], axis=1)
    return paired

def forward_layer(signal, weight, bias_conv, gain_row, bias_row, kernel_taps):
    patches = make_patches(signal, kernel_taps)
    conv_out = jnp.dot(patches, weight, preferred_element_type=jnp.float32) + bias_conv
    center = lax.optimization_barrier(jnp.mean(conv_out, axis=1, keepdims=True))
    centered = conv_out - center
    inverse = lax.rsqrt(lax.optimization_barrier(jnp.mean(centered * centered, axis=1, keepdims=True)) + EPSILON)
    normed = centered * inverse
    preact = normed * gain_row + bias_row
    return (gelu_exact(preact).astype(jnp.bfloat16), (patches, normed, preact, inverse))

def backward_layer(grad_act, weight, gain_row, stored, kernel_taps):
    patches, normed, preact, inverse = stored
    grad_normed = grad_act.astype(jnp.float32) * gelu_slope(preact) * gain_row
    avg_grad = lax.optimization_barrier(jnp.mean(grad_normed, axis=1, keepdims=True))
    avg_cross = lax.optimization_barrier(jnp.mean(grad_normed * normed, axis=1, keepdims=True))
    grad_conv = (inverse * (grad_normed - avg_grad - normed * avg_cross)).astype(jnp.bfloat16)
    weight_grad = jnp.dot(patches.T, grad_conv, preferred_element_type=jnp.float32)
    grad_patch = jnp.dot(grad_conv, weight.T, preferred_element_type=jnp.float32)
    channels = weight.shape[1]
    if kernel_taps == 3:
        tail = grad_patch[:, 2 * channels:]
        shifted = jnp.concatenate([jnp.zeros((1, channels), jnp.float32), tail[:-1]], axis=0)
        grad_patch = jnp.concatenate([grad_patch[:, :channels] + shifted, grad_patch[:, channels:2 * channels]], axis=1)
    return (grad_patch.reshape(-1, channels).astype(jnp.bfloat16), weight_grad)

def reference(features, conv_wide, conv_narrow, conv_bias, norm_gain, norm_bias, proj_gain, proj_weight, proj_bias, upstream):
    conv_weights = (conv_wide, conv_narrow)
    kernel_list = (3, 2)
    grad_heads = upstream.reshape(RECORDINGS, HEADS, FRAMES, HEAD_DIM)

    def one_recording(totals, inputs):
        signal, grad_piece = inputs
        stored_all = []
        for position in range(LAYERS):
            signal, stored = forward_layer(signal, conv_weights[position], conv_bias[position], norm_gain[position], norm_bias[position], kernel_list[position])
            stored_all.append(stored)
        widened = signal.astype(jnp.float32)
        centered = widened - lax.optimization_barrier(jnp.mean(widened, axis=1, keepdims=True))
        row_inverse = lax.rsqrt(lax.optimization_barrier(jnp.mean(centered * centered, axis=1, keepdims=True)) + EPSILON)
        unit_rows = centered * row_inverse
        normed_in = (unit_rows * proj_gain).astype(jnp.bfloat16)
        projected = (jnp.dot(normed_in, proj_weight, preferred_element_type=jnp.float32) + proj_bias).astype(jnp.bfloat16)
        heads_out = projected.reshape(FRAMES, HEADS, HEAD_DIM).transpose(1, 0, 2)
        grad_frames = grad_piece.transpose(1, 0, 2).reshape(FRAMES, WIDTH)
        grad_unit = jnp.dot(grad_frames, proj_weight.T, preferred_element_type=jnp.float32) * proj_gain
        grad_signal = (row_inverse * (grad_unit - lax.optimization_barrier(jnp.mean(grad_unit, axis=1, keepdims=True)) - unit_rows * lax.optimization_barrier(jnp.mean(grad_unit * unit_rows, axis=1, keepdims=True)))).astype(jnp.bfloat16)
        layer_grads = []
        for position in reversed(range(LAYERS)):
            grad_signal, weight_grad = backward_layer(grad_signal, conv_weights[position], norm_gain[position], stored_all[position], kernel_list[position])
            layer_grads.append(weight_grad)
        new_totals = (totals[0] + layer_grads[1], totals[1] + layer_grads[0])
        return (new_totals, (heads_out, grad_signal))
    initial = (jnp.zeros(conv_wide.shape, jnp.float32), jnp.zeros(conv_narrow.shape, jnp.float32))
    totals, outputs = lax.scan(one_recording, initial, (features, grad_heads))
    heads_all, grad_all = outputs
    factor = 1.0 / math.sqrt(RECORDINGS * FRAMES)
    attn_input = heads_all.reshape(RECORDINGS * HEADS, FRAMES, HEAD_DIM)
    return (attn_input, grad_all, (totals[0] * factor).reshape(-1), (totals[1] * factor).reshape(-1))
```

```python
import math

import jax
import jax.numpy as jnp
from jax import lax
from jax.experimental import pallas as pl
from jax.experimental.pallas import tpu as pltpu
from jax.sharding import PartitionSpec as P

HEADS = 16
HEAD_DIM = 120


EPSILON = 1e-05
SQRT_HALF = 0.7071067811865476
INV_ROOT_TAU = 0.3989422804014327


def passed_along(value, axis, steps):
    count = lax.axis_size(axis)
    leading, last = (max(0, -steps), min(count, count - steps))
    return lax.ppermute(value, axis, [(source, source + steps) for source in range(leading, last)])


def gelu_exact(values):
    return 0.5 * values * (1.0 + lax.erf(values * SQRT_HALF))


def gelu_slope(values):
    cumulative = 0.5 * (1.0 + lax.erf(values * SQRT_HALF))
    density = jnp.exp(-0.5 * values * values) * INV_ROOT_TAU
    return cumulative + values * density


def wide_patches(signal, first_next):
    recs_local, length, channels = signal.shape
    paired = signal.reshape(recs_local, length // 2, 2 * channels)
    following = jnp.concatenate([paired[:, 1:, :channels], first_next], axis=1)
    return jnp.concatenate([paired, following], axis=2)


def narrow_patches(signal):
    recs_local, length, channels = signal.shape
    return signal.reshape(recs_local, length // 2, 2 * channels)


def conv_forward(patches, weight, bias_conv, gain_row, bias_row):
    recs_local, out_rows, patch_width = patches.shape
    conv_out = jnp.dot(
        patches.reshape(recs_local * out_rows, patch_width),
        weight,
        preferred_element_type=jnp.float32,
    )
    conv_out = conv_out.reshape(recs_local, out_rows, weight.shape[1]) + bias_conv
    center = jnp.mean(conv_out, axis=2, keepdims=True)
    centered = conv_out - center
    inverse = lax.rsqrt(jnp.mean(centered * centered, axis=2, keepdims=True) + EPSILON)
    normed = centered * inverse
    preact = normed * gain_row + bias_row
    activated = gelu_exact(preact).astype(jnp.bfloat16)
    return (activated, (patches, normed, preact, inverse))


def conv_backward(grad_act, weight, gain_row, stored):
    patches, normed, preact, inverse = stored
    recs_local, out_rows, patch_width = patches.shape
    grad_normed = grad_act.astype(jnp.float32) * gelu_slope(preact) * gain_row
    avg_grad = jnp.mean(grad_normed, axis=2, keepdims=True)
    avg_cross = jnp.mean(grad_normed * normed, axis=2, keepdims=True)
    grad_conv = (inverse * (grad_normed - avg_grad - normed * avg_cross)).astype(jnp.bfloat16)
    flat_patches = patches.reshape(recs_local * out_rows, patch_width)
    flat_grad = grad_conv.reshape(recs_local * out_rows, weight.shape[1])
    weight_grad = lax.dot_general(
        flat_patches, flat_grad, (((0,), (0,)), ((), ())), preferred_element_type=jnp.float32
    )
    grad_patch = lax.dot_general(
        flat_grad, weight, (((1,), (1,)), ((), ())), preferred_element_type=jnp.float32
    )
    return (weight_grad, grad_patch.reshape(recs_local, out_rows, patch_width))


def wide_input_grad(grad_patch, channels):
    recs_local, out_rows, patch_width = grad_patch.shape
    tail = grad_patch[:, :, 2 * channels :]
    incoming = passed_along(tail[:, -1:], "tm", 1)
    shifted = jnp.concatenate([incoming, tail[:, :-1]], axis=1)
    first_half = grad_patch[:, :, :channels] + shifted
    combined = jnp.concatenate([first_half, grad_patch[:, :, channels : 2 * channels]], axis=2)
    return combined.reshape(recs_local, 2 * out_rows, channels).astype(jnp.bfloat16)


def narrow_input_grad(grad_patch, channels):
    recs_local, out_rows, patch_width = grad_patch.shape
    return grad_patch.reshape(recs_local, 2 * out_rows, channels).astype(jnp.bfloat16)


def share_grad(weight_grad, factor):
    flat = (weight_grad * factor).reshape(-1)
    result = lax.psum_scatter(flat, ("dp", "tm"), scatter_dimension=0, tiled=True)
    return result


def generic_shards(
    features,
    conv_wide,
    conv_narrow,
    conv_bias,
    norm_gain,
    norm_bias,
    proj_gain,
    proj_weight,
    proj_bias,
    upstream,
):
    recs_local, length, channels = features.shape
    tm_count = lax.axis_size("tm")
    frames_total = upstream.shape[1]
    frames_local = frames_total // tm_count
    factor = 1.0 / math.sqrt(recs_local * lax.axis_size("dp") * frames_total)
    grad_frames = lax.all_to_all(upstream, "tm", split_axis=1, concat_axis=0, tiled=True)
    first_next = passed_along(features[:, :1], "tm", -1)
    act_wide, stored_wide = conv_forward(
        wide_patches(features, first_next), conv_wide, conv_bias[0], norm_gain[0], norm_bias[0]
    )
    act_narrow, stored_narrow = conv_forward(
        narrow_patches(act_wide), conv_narrow, conv_bias[1], norm_gain[1], norm_bias[1]
    )
    widened = act_narrow.astype(jnp.float32)
    centered = widened - jnp.mean(widened, axis=2, keepdims=True)
    row_inverse = lax.rsqrt(jnp.mean(centered * centered, axis=2, keepdims=True) + EPSILON)
    unit_rows = centered * row_inverse
    normed_in = (unit_rows * proj_gain).astype(jnp.bfloat16)
    weight_heads = proj_weight.reshape(channels, HEADS, HEAD_DIM)
    projected = jnp.einsum(
        "rfc,chd->rhfd", normed_in, weight_heads, preferred_element_type=jnp.float32
    ) + proj_bias.reshape(HEADS, 1, HEAD_DIM)
    heads_local = projected.astype(jnp.bfloat16).reshape(recs_local * HEADS, frames_local, HEAD_DIM)
    attn_input = lax.all_to_all(heads_local, "tm", split_axis=0, concat_axis=1, tiled=True)
    grad_heads = grad_frames.reshape(recs_local, HEADS, frames_local, HEAD_DIM)
    grad_unit = (
        jnp.einsum("rhfd,chd->rfc", grad_heads, weight_heads, preferred_element_type=jnp.float32)
        * proj_gain
    )
    grad_last = (
        row_inverse
        * (
            grad_unit
            - jnp.mean(grad_unit, axis=2, keepdims=True)
            - unit_rows * jnp.mean(grad_unit * unit_rows, axis=2, keepdims=True)
        )
    ).astype(jnp.bfloat16)
    weight_narrow, patch_narrow = conv_backward(grad_last, conv_narrow, norm_gain[1], stored_narrow)
    grad_conv_narrow = share_grad(weight_narrow, factor)
    grad_first = narrow_input_grad(patch_narrow, channels)
    weight_wide, patch_wide = conv_backward(grad_first, conv_wide, norm_gain[0], stored_wide)
    grad_conv_wide = share_grad(weight_wide, factor)
    feature_grad = wide_input_grad(patch_wide, channels)
    return (attn_input, feature_grad, grad_conv_wide, grad_conv_narrow)


F32 = jnp.float32
BF16 = jnp.bfloat16
NT = (((1,), (1,)), ((), ()))


def dot(a, b):
    return jnp.dot(a, b, preferred_element_type=F32)


def dot_nt(a, b):
    return lax.dot_general(a, b, NT, preferred_element_type=F32)


def row_mean(values):
    return jnp.mean(values, axis=1, keepdims=True)


def normalized(values):
    centered = values - row_mean(values)
    inverse = lax.rsqrt(row_mean(centered * centered) + EPSILON)
    return centered * inverse, inverse


def gelu_parts(preact):
    cumulative = 0.5 * (1.0 + lax.erf(preact * SQRT_HALF))
    slope = cumulative + preact * (jnp.exp(-0.5 * preact * preact) * INV_ROOT_TAU)
    return preact * cumulative, slope


def params(limit=58):
    return pltpu.CompilerParams(vmem_limit_bytes=limit << 20)


def shaped(*shapes):
    return [jax.ShapeDtypeStruct(shape, dtype) for shape, dtype in shapes]


def move_slices(source, shape, slices, views):
    def kernel(src, dst, sems):
        copies = []
        for k in range(slices):
            from_at, to_at = views(k)
            copies.append(pltpu.make_async_copy(src.at[from_at], dst.at[to_at], sems.at[k]))
        for copy in copies:
            copy.start()
        for copy in copies:
            copy.wait()

    return pl.pallas_call(
        kernel,
        out_shape=jax.ShapeDtypeStruct(shape, source.dtype),
        in_specs=[pl.BlockSpec(memory_space=pl.ANY)],
        out_specs=pl.BlockSpec(memory_space=pl.ANY),
        scratch_shapes=[pltpu.SemaphoreType.DMA((slices,))],
        name="move_slices",
    )(source)


def spread_rows(spread, first, count):
    lanes = [spread[lane, pl.ds(first, count, stride=4), :] for lane in range(spread.shape[0])]
    return jnp.concatenate(lanes, axis=1)


def put_rows(spread, first, value):
    for lane in range(spread.shape[0]):
        spread[lane, pl.ds(first, value.shape[0], stride=4), :] = value[:, lane * 128 : (lane + 1) * 128]


def forward_kernel(
    feat,
    halo,
    conv_wide,
    conv_narrow,
    conv_bias,
    norm_gain,
    norm_bias,
    proj_gain,
    proj_weight,
    proj_bias,
    proj_t,
    patch_t,
    act_t,
    normed_w,
    slope_w,
    inv_w,
    normed_n,
    slope_n,
    inv_n,
    unit_out,
    row_inv,
    spread,
    patches,
):
    frames = feat.shape[0] // 4
    channels = feat.shape[1]
    for lane in range(channels // 128):
        spread[lane] = feat[:, lane * 128 : (lane + 1) * 128].astype(F32)
    rows = [spread_rows(spread, j, frames) for j in range(4)]
    following = pltpu.roll(rows[0], frames - 1, axis=0)
    at_end = lax.broadcasted_iota(jnp.int32, (frames, 1), 0) == frames - 1
    rows.append(jnp.where(at_end, halo[0:1, :].astype(F32), following))
    rows = [row.astype(BF16) for row in rows]
    for parity in range(2):
        for tap in range(3):
            piece = rows[2 * parity + tap]
            patches[parity * frames : (parity + 1) * frames, tap * channels : (tap + 1) * channels] = piece
            patch_t[tap * channels : (tap + 1) * channels, parity * frames : (parity + 1) * frames] = piece.T
    conv = dot(patches[...], conv_wide[...]) + conv_bias[0:1, :]
    normed, inverse = normalized(conv)
    normed_w[...] = normed
    inv_w[...] = jnp.broadcast_to(inverse, inv_w.shape)
    act, slope = gelu_parts(normed * norm_gain[0:1, :] + norm_bias[0:1, :])
    slope_w[...] = slope * norm_gain[0:1, :]
    act = act.astype(BF16)
    even, odd = act[:frames], act[frames:]
    act_t[0:channels, :] = even.T
    act_t[channels:, :] = odd.T
    conv = dot(even, conv_narrow[0:channels, :]) + dot(odd, conv_narrow[channels:, :]) + conv_bias[1:2, :]
    normed, inverse = normalized(conv)
    normed_n[...] = normed
    inv_n[...] = jnp.broadcast_to(inverse, inv_n.shape)
    act, slope = gelu_parts(normed * norm_gain[1:2, :] + norm_bias[1:2, :])
    slope_n[...] = slope * norm_gain[1:2, :]
    unit, inverse = normalized(act.astype(BF16).astype(F32))
    unit_out[...] = unit
    row_inv[...] = jnp.broadcast_to(inverse, row_inv.shape)
    normed_in = (unit * proj_gain[...]).astype(BF16)
    projected = dot(normed_in, proj_weight[...]) + proj_bias[...]
    proj_t[...] = projected.astype(BF16).T


def backward_kernel(
    factor,
    grad_t,
    proj_weight,
    proj_gain,
    conv_narrow,
    last_tap,
    patch_t,
    act_t,
    normed_w,
    slope_w,
    inv_w,
    normed_n,
    slope_n,
    inv_n,
    unit_in,
    row_inv,
    send,
    keep,
    grad_conv,
    tail,
):
    frames, channels = unit_in.shape
    core = lax.axis_index("dp") % 2
    unit = unit_in[...]
    grad_unit = dot(proj_weight[...], grad_t[...]).T * proj_gain[...]
    grad_last = row_inv[:, 0:1] * (grad_unit - row_mean(grad_unit) - unit * row_mean(grad_unit * unit))
    grad_normed = grad_last.astype(BF16).astype(F32) * slope_n[...]
    normed = normed_n[...]
    grad_narrow = (
        inv_n[:, 0:1] * (grad_normed - row_mean(grad_normed) - normed * row_mean(grad_normed * normed))
    ).astype(BF16)
    grad_even = dot_nt(grad_narrow, conv_narrow[0:channels, :])
    grad_odd = dot_nt(grad_narrow, conv_narrow[channels:, :])
    grad_first = jnp.concatenate([grad_even, grad_odd], axis=0).astype(BF16)
    grad_normed = grad_first.astype(F32) * slope_w[...]
    normed = normed_w[...]
    grad_wide = (
        inv_w[:, 0:1] * (grad_normed - row_mean(grad_normed) - normed * row_mean(grad_normed * normed))
    ).astype(BF16)
    grad_conv[...] = grad_wide
    tail[...] = dot_nt(grad_wide[2 * frames - 8 :, :], last_tap[...])
    outer = send.shape[0]
    inner = send.shape[1]
    for target, owner in ((send, 1 - core), (keep, core)):
        for block in range(outer):
            row = 0
            for lhs, rhs in ((patch_t, grad_wide), (act_t, grad_narrow)):
                part = lhs.shape[0] // (2 * outer)
                start = pl.multiple_of((2 * block + owner) * part, part)
                value = (dot(lhs[pl.ds(start, part), :], rhs) * factor).astype(BF16)
                each = part // inner
                for k in range(inner):
                    target[block, k, row : row + each, :] = value[k * each : (k + 1) * each]
                row += each


def input_grad_kernel(grad_conv, conv_wide, incoming, out, spread):
    frames = grad_conv.shape[0] // 2
    channels = grad_conv.shape[1]
    even, odd = grad_conv[:frames, :], grad_conv[frames:, :]
    taps = [conv_wide[tap * channels : (tap + 1) * channels, :] for tap in range(3)]
    shifted = pltpu.roll(dot_nt(odd, taps[2]), 1, axis=0)
    at_start = lax.broadcasted_iota(jnp.int32, (frames, 1), 0) == 0
    shifted = jnp.where(at_start, incoming[7:8, :], shifted)
    put_rows(spread, 0, dot_nt(even, taps[0]) + shifted)
    put_rows(spread, 1, dot_nt(even, taps[1]))
    put_rows(spread, 2, dot_nt(even, taps[2]) + dot_nt(odd, taps[0]))
    put_rows(spread, 3, dot_nt(odd, taps[1]))
    for lane in range(channels // 128):
        out[:, lane * 128 : (lane + 1) * 128] = spread[lane].astype(BF16)


def first_sum_kernel(keep, received, *outs):
    y = lax.axis_index("dp") // 2
    x = lax.axis_index("tm") % 2
    inner = keep.shape[1] // 2
    for flip, out in enumerate(outs):
        block = y ^ (flip // 2)
        lane = x ^ (flip % 2)
        for z in range(inner):
            at = 2 * z + lane
            out[z] = (keep[block, at].astype(F32) + received[block, at].astype(F32)).astype(BF16)


def second_sum_kernel(a, b, c, d, *outs):
    z = lax.axis_index("tm") // 2
    for flip, out in enumerate(outs):
        at = z ^ flip
        total = (a[at].astype(F32) + b[at].astype(F32)) + (c[at].astype(F32) + d[at].astype(F32))
        out[...] = total.astype(BF16)


def last_sum_kernel(wide_rows, a, b, c, d, wide, narrow):
    total = (a[...].astype(F32) + b[...].astype(F32)) + (c[...].astype(F32) + d[...].astype(F32))
    rows, channels = total.shape
    pieces = channels // 128
    for p in range(pieces):
        lanes = total[:, p * 128 : (p + 1) * 128]
        wide[pl.ds(p, wide_rows, stride=pieces), :] = lanes[:wide_rows]
        narrow[pl.ds(p, rows - wide_rows, stride=pieces), :] = lanes[wide_rows:]


def flipped(dy, dc, dz, dx):
    dp, tm = lax.axis_size("dp"), lax.axis_size("tm")
    change_dp, change_tm = 2 * dy + dc, 2 * dz + dx
    return [
        (p * tm + t, (p ^ change_dp) * tm + (t ^ change_tm)) for p in range(dp) for t in range(tm)
    ]


def swap(value, dy, dc, dz, dx):
    return lax.ppermute(value, ("dp", "tm"), flipped(dy, dc, dz, dx))


def shards(
    features,
    conv_wide,
    conv_narrow,
    conv_bias,
    norm_gain,
    norm_bias,
    proj_gain,
    proj_weight,
    proj_bias,
    upstream,
):
    dp, tm = lax.axis_size("dp"), lax.axis_size("tm")
    recs_local, length, channels = features.shape
    pairs, frames_total, depth = upstream.shape
    frames = frames_total // tm
    if not (dp == 4 and tm == 8 and recs_local == 1 and frames % 128 == 0 and pairs * tm == HEADS):
        return generic_shards(
            features,
            conv_wide,
            conv_narrow,
            conv_bias,
            norm_gain,
            norm_bias,
            proj_gain,
            proj_weight,
            proj_bias,
            upstream,
        )
    width = HEADS * depth
    factor = 1.0 / math.sqrt(recs_local * dp * frames_total)
    ups = upstream.transpose(0, 2, 1)
    packed = move_slices(
        ups,
        (tm, pairs, depth, frames),
        tm,
        lambda k: ((slice(None), slice(None), pl.ds(k * frames, frames)), k),
    )
    grad_t = lax.all_to_all(
        packed.reshape(tm, pairs * depth, frames), "tm", split_axis=0, concat_axis=0, tiled=True
    ).reshape(width, frames)
    signal = features.reshape(length, channels)
    halo = passed_along(signal[:8], "tm", -1)
    wide_rows = 2 * frames
    saved = shaped(
        ((3 * channels, wide_rows), BF16),
        ((2 * channels, frames), BF16),
        ((wide_rows, channels), F32),
        ((wide_rows, channels), F32),
        ((wide_rows, 128), F32),
        ((frames, channels), F32),
        ((frames, channels), F32),
        ((frames, 128), F32),
        ((frames, channels), F32),
        ((frames, 128), F32),
    )
    proj_t, *stored = pl.pallas_call(
        forward_kernel,
        out_shape=shaped(((width, frames), BF16)) + saved,
        scratch_shapes=[pltpu.VMEM((channels // 128, length, 128), F32), pltpu.VMEM((wide_rows, 3 * channels), BF16)],
        compiler_params=params(),
        name="forward",
    )(
        signal,
        halo,
        conv_wide,
        conv_narrow,
        conv_bias,
        norm_gain,
        norm_bias,
        proj_gain.reshape(1, channels),
        proj_weight,
        proj_bias.reshape(1, width),
    )
    proj_t, grad_t = lax.optimization_barrier((proj_t, grad_t))
    outer, inner = dp // 2, tm
    part_rows = 5 * channels // (dp * tm)
    part = ((outer, inner, part_rows, channels), BF16)
    send, keep, grad_conv, tail = pl.pallas_call(
        lambda *refs: backward_kernel(factor, *refs),
        out_shape=shaped(part, part, ((wide_rows, channels), BF16), ((8, channels), F32)),
        compiler_params=params(),
        name="backward",
    )(
        grad_t,
        proj_weight,
        proj_gain.reshape(1, channels),
        conv_narrow,
        conv_wide[2 * channels :],
        *stored,
    )
    received = swap(send, 0, 1, 0, 0)
    heads = lax.all_to_all(
        proj_t.reshape(tm, pairs * depth, frames), "tm", split_axis=0, concat_axis=0, tiled=True
    )
    attn_t = move_slices(
        heads.reshape(tm, pairs, depth, frames),
        (pairs, depth, frames_total),
        tm,
        lambda k: (k, (slice(None), slice(None), pl.ds(k * frames, frames))),
    )
    attn_input = attn_t.transpose(0, 2, 1)
    incoming = passed_along(tail, "tm", 1)
    feature_grad = pl.pallas_call(
        input_grad_kernel,
        out_shape=jax.ShapeDtypeStruct((length, channels), BF16),
        scratch_shapes=[pltpu.VMEM((channels // 128, length, 128), F32)],
        compiler_params=params(),
        name="input_grad",
    )(grad_conv, conv_wide, incoming)
    plane = ((tm // 2, part_rows, channels), BF16)
    own, *outgoing = pl.pallas_call(
        first_sum_kernel,
        out_shape=shaped(plane, plane, plane, plane),
        compiler_params=params(),
        name="first_sum",
    )(keep, received)
    arrived = [swap(value, k // 2, 0, 0, k % 2) for k, value in enumerate(outgoing, 1)]
    piece = ((part_rows, channels), BF16)
    own, *outgoing = pl.pallas_call(
        second_sum_kernel,
        out_shape=shaped(piece, piece, piece, piece),
        compiler_params=params(),
        name="second_sum",
    )(own, *arrived)
    arrived = [swap(value, 0, 0, k, 0) for k, value in enumerate(outgoing, 1)]
    own_wide = 3 * channels // (dp * tm)
    wide, narrow = pl.pallas_call(
        lambda *refs: last_sum_kernel(own_wide, *refs),
        out_shape=shaped(
            ((own_wide * channels // 128, 128), F32),
            (((part_rows - own_wide) * channels // 128, 128), F32),
        ),
        compiler_params=params(),
        name="last_sum",
    )(own, *arrived)
    return (
        attn_input,
        feature_grad.reshape(recs_local, length, channels),
        wide.reshape(-1),
        narrow.reshape(-1),
    )


def solution(mesh):
    in_specs = (
        P("dp", "tm", None),
        P(),
        P(),
        P(),
        P(),
        P(),
        P(),
        P(),
        P(),
        P(("dp", "tm"), None, None),
    )
    out_specs = (P(("dp", "tm"), None, None), P("dp", "tm", None), P(("dp", "tm")), P(("dp", "tm")))
    return jax.shard_map(shards, mesh=mesh, in_specs=in_specs, out_specs=out_specs, check_vma=False)
```

```python
import math

import jax
import jax.numpy as jnp
from jax import lax
from jax.experimental import pallas as pl
from jax.experimental.pallas import tpu as pltpu
from jax.sharding import PartitionSpec as P

HEADS = 16
HEAD_DIM = 120


EPSILON = 1e-05
SQRT_HALF = 0.7071067811865476
INV_ROOT_TAU = 0.3989422804014327


def passed_along(value, axis, steps):
    count = lax.axis_size(axis)
    leading, last = (max(0, -steps), min(count, count - steps))
    return lax.ppermute(value, axis, [(source, source + steps) for source in range(leading, last)])


def gelu_exact(values):
    return 0.5 * values * (1.0 + lax.erf(values * SQRT_HALF))


def gelu_slope(values):
    cumulative = 0.5 * (1.0 + lax.erf(values * SQRT_HALF))
    density = jnp.exp(-0.5 * values * values) * INV_ROOT_TAU
    return cumulative + values * density


def wide_patches(signal, first_next):
    recs_local, length, channels = signal.shape
    paired = signal.reshape(recs_local, length // 2, 2 * channels)
    following = jnp.concatenate([paired[:, 1:, :channels], first_next], axis=1)
    return jnp.concatenate([paired, following], axis=2)


def narrow_patches(signal):
    recs_local, length, channels = signal.shape
    return signal.reshape(recs_local, length // 2, 2 * channels)


def conv_forward(patches, weight, bias_conv, gain_row, bias_row):
    recs_local, out_rows, patch_width = patches.shape
    conv_out = jnp.dot(
        patches.reshape(recs_local * out_rows, patch_width),
        weight,
        preferred_element_type=jnp.float32,
    )
    conv_out = conv_out.reshape(recs_local, out_rows, weight.shape[1]) + bias_conv
    center = jnp.mean(conv_out, axis=2, keepdims=True)
    centered = conv_out - center
    inverse = lax.rsqrt(jnp.mean(centered * centered, axis=2, keepdims=True) + EPSILON)
    normed = centered * inverse
    preact = normed * gain_row + bias_row
    activated = gelu_exact(preact).astype(jnp.bfloat16)
    return (activated, (patches, normed, preact, inverse))


def conv_backward(grad_act, weight, gain_row, stored):
    patches, normed, preact, inverse = stored
    recs_local, out_rows, patch_width = patches.shape
    grad_normed = grad_act.astype(jnp.float32) * gelu_slope(preact) * gain_row
    avg_grad = jnp.mean(grad_normed, axis=2, keepdims=True)
    avg_cross = jnp.mean(grad_normed * normed, axis=2, keepdims=True)
    grad_conv = (inverse * (grad_normed - avg_grad - normed * avg_cross)).astype(jnp.bfloat16)
    flat_patches = patches.reshape(recs_local * out_rows, patch_width)
    flat_grad = grad_conv.reshape(recs_local * out_rows, weight.shape[1])
    weight_grad = lax.dot_general(
        flat_patches, flat_grad, (((0,), (0,)), ((), ())), preferred_element_type=jnp.float32
    )
    grad_patch = lax.dot_general(
        flat_grad, weight, (((1,), (1,)), ((), ())), preferred_element_type=jnp.float32
    )
    return (weight_grad, grad_patch.reshape(recs_local, out_rows, patch_width))


def wide_input_grad(grad_patch, channels):
    recs_local, out_rows, patch_width = grad_patch.shape
    tail = grad_patch[:, :, 2 * channels :]
    incoming = passed_along(tail[:, -1:], "tm", 1)
    shifted = jnp.concatenate([incoming, tail[:, :-1]], axis=1)
    first_half = grad_patch[:, :, :channels] + shifted
    combined = jnp.concatenate([first_half, grad_patch[:, :, channels : 2 * channels]], axis=2)
    return combined.reshape(recs_local, 2 * out_rows, channels).astype(jnp.bfloat16)


def narrow_input_grad(grad_patch, channels):
    recs_local, out_rows, patch_width = grad_patch.shape
    return grad_patch.reshape(recs_local, 2 * out_rows, channels).astype(jnp.bfloat16)


def share_grad(weight_grad, factor):
    flat = (weight_grad * factor).reshape(-1)
    result = lax.psum_scatter(flat, ("dp", "tm"), scatter_dimension=0, tiled=True)
    return result


def generic_shards(
    features,
    conv_wide,
    conv_narrow,
    conv_bias,
    norm_gain,
    norm_bias,
    proj_gain,
    proj_weight,
    proj_bias,
    upstream,
):
    recs_local, length, channels = features.shape
    tm_count = lax.axis_size("tm")
    frames_total = upstream.shape[1]
    frames_local = frames_total // tm_count
    factor = 1.0 / math.sqrt(recs_local * lax.axis_size("dp") * frames_total)
    grad_frames = lax.all_to_all(upstream, "tm", split_axis=1, concat_axis=0, tiled=True)
    first_next = passed_along(features[:, :1], "tm", -1)
    act_wide, stored_wide = conv_forward(
        wide_patches(features, first_next), conv_wide, conv_bias[0], norm_gain[0], norm_bias[0]
    )
    act_narrow, stored_narrow = conv_forward(
        narrow_patches(act_wide), conv_narrow, conv_bias[1], norm_gain[1], norm_bias[1]
    )
    widened = act_narrow.astype(jnp.float32)
    centered = widened - jnp.mean(widened, axis=2, keepdims=True)
    row_inverse = lax.rsqrt(jnp.mean(centered * centered, axis=2, keepdims=True) + EPSILON)
    unit_rows = centered * row_inverse
    normed_in = (unit_rows * proj_gain).astype(jnp.bfloat16)
    weight_heads = proj_weight.reshape(channels, HEADS, HEAD_DIM)
    projected = jnp.einsum(
        "rfc,chd->rhfd", normed_in, weight_heads, preferred_element_type=jnp.float32
    ) + proj_bias.reshape(HEADS, 1, HEAD_DIM)
    heads_local = projected.astype(jnp.bfloat16).reshape(recs_local * HEADS, frames_local, HEAD_DIM)
    attn_input = lax.all_to_all(heads_local, "tm", split_axis=0, concat_axis=1, tiled=True)
    grad_heads = grad_frames.reshape(recs_local, HEADS, frames_local, HEAD_DIM)
    grad_unit = (
        jnp.einsum("rhfd,chd->rfc", grad_heads, weight_heads, preferred_element_type=jnp.float32)
        * proj_gain
    )
    grad_last = (
        row_inverse
        * (
            grad_unit
            - jnp.mean(grad_unit, axis=2, keepdims=True)
            - unit_rows * jnp.mean(grad_unit * unit_rows, axis=2, keepdims=True)
        )
    ).astype(jnp.bfloat16)
    weight_narrow, patch_narrow = conv_backward(grad_last, conv_narrow, norm_gain[1], stored_narrow)
    grad_conv_narrow = share_grad(weight_narrow, factor)
    grad_first = narrow_input_grad(patch_narrow, channels)
    weight_wide, patch_wide = conv_backward(grad_first, conv_wide, norm_gain[0], stored_wide)
    grad_conv_wide = share_grad(weight_wide, factor)
    feature_grad = wide_input_grad(patch_wide, channels)
    return (attn_input, feature_grad, grad_conv_wide, grad_conv_narrow)


F32 = jnp.float32
BF16 = jnp.bfloat16
NT = (((1,), (1,)), ((), ()))


def dot(a, b):
    return jnp.dot(a, b, preferred_element_type=F32)


def dot_nt(a, b):
    return lax.dot_general(a, b, NT, preferred_element_type=F32)


def row_mean(values):
    return jnp.mean(values, axis=1, keepdims=True)


def normalized(values):
    centered = values - row_mean(values)
    inverse = lax.rsqrt(row_mean(centered * centered) + EPSILON)
    return centered * inverse, inverse


def gelu_parts(preact):
    cumulative = 0.5 * (1.0 + lax.erf(preact * SQRT_HALF))
    slope = cumulative + preact * (jnp.exp(-0.5 * preact * preact) * INV_ROOT_TAU)
    return preact * cumulative, slope


def local(kernel, operands, outs, name, limit=16, scratch=(), raw=(), raw_out=(), aliases=None, cost=1000):
    out_shape, out_specs = [], []
    for number, (shape, dtype, stays) in enumerate(outs):
        out_shape.append((pltpu.VMEM if stays else pltpu.HBM)(shape, dtype))
        out_specs.append(pl.BlockSpec(memory_space=pltpu.HBM if number in raw_out else pltpu.VMEM))
    held = [
        pltpu.with_memory_space_constraint(x, pltpu.HBM if k in raw else pltpu.VMEM)
        for k, x in enumerate(operands)
    ]
    return pl.pallas_call(
        kernel,
        out_shape=out_shape,
        in_specs=[
            pl.BlockSpec(memory_space=pltpu.HBM if k in raw else pltpu.VMEM) for k in range(len(operands))
        ],
        out_specs=out_specs,
        scratch_shapes=list(scratch),
        input_output_aliases=aliases or {},
        compiler_params=pltpu.CompilerParams(vmem_limit_bytes=limit << 20),
        cost_estimate=pl.CostEstimate(flops=cost, bytes_accessed=0, transcendentals=0),
        name=name,
    )(*held)


def run_copies(pairs, sems):
    copies = [pltpu.make_async_copy(src, dst, sems.at[k]) for k, (src, dst) in enumerate(pairs)]
    for copy in copies:
        copy.start()
    for copy in copies:
        copy.wait()


def cut_kernel(whole, *refs):
    *parts, held, sems, out_sems = refs
    count, width = held.shape[0], held.shape[3]
    own = lax.axis_index("tm")
    reads, writes = [], []
    for k in range(count):
        start = pl.multiple_of((own ^ k) * width, width)
        reads.append(pltpu.make_async_copy(whole.at[:, :, pl.ds(start, width)], held.at[k], sems.at[k]))
        writes.append(pltpu.make_async_copy(held.at[k], parts[k], out_sems.at[k]))
    for read in reads:
        read.start()
    for read, write in zip(reads, writes):
        read.wait()
        write.start()
    for write in writes:
        write.wait()


def join_kernel(parts, whole, sems):
    width = parts.shape[3]
    run_copies([(parts.at[k], whole.at[:, :, pl.ds(k * width, width)]) for k in range(parts.shape[0])], sems)


class Loads:
    def __init__(self, sources, held, sems):
        self.pairs = [
            (pltpu.make_async_copy(src, buf, sems.at[k]), buf) for k, (src, buf) in enumerate(zip(sources, held))
        ]
        for read, _ in self.pairs:
            read.start()

    def take(self, count):
        taken, self.pairs = self.pairs[:count], self.pairs[count:]
        for read, _ in taken:
            read.wait()
        return [buf for _, buf in taken]


def spread_rows(spread, first, count):
    lanes = [spread[lane, pl.ds(first, count, stride=4), :] for lane in range(spread.shape[0])]
    return jnp.concatenate(lanes, axis=1)


def put_rows(spread, first, value):
    for lane in range(spread.shape[0]):
        spread[lane, pl.ds(first, value.shape[0], stride=4), :] = value[:, lane * 128 : (lane + 1) * 128]


def forward_kernel(*refs):
    sources, outs, rest = refs[:10], refs[10:21], refs[21:]
    *held, sems, spread, patches = rest
    (
        proj_t,
        patch_t,
        act_t,
        normed_w,
        slope_w,
        inv_w,
        normed_n,
        slope_n,
        inv_n,
        unit_out,
        row_inv,
    ) = outs
    loads = Loads(sources, held, sems)
    feat, halo, conv_bias, norm_gain, norm_bias = loads.take(5)
    frames = feat.shape[0] // 4
    channels = feat.shape[1]
    for lane in range(channels // 128):
        spread[lane] = feat[:, lane * 128 : (lane + 1) * 128].astype(F32)
    rows = [spread_rows(spread, j, frames) for j in range(4)]
    following = pltpu.roll(rows[0], frames - 1, axis=0)
    at_end = lax.broadcasted_iota(jnp.int32, (frames, 1), 0) == frames - 1
    rows.append(jnp.where(at_end, halo[0:1, :].astype(F32), following))
    rows = [row.astype(BF16) for row in rows]
    for parity in range(2):
        for tap in range(3):
            piece = rows[2 * parity + tap]
            patches[parity * frames : (parity + 1) * frames, tap * channels : (tap + 1) * channels] = piece
            patch_t[tap * channels : (tap + 1) * channels, parity * frames : (parity + 1) * frames] = piece.T
    (conv_wide,) = loads.take(1)
    conv = dot(patches[...], conv_wide[...]) + conv_bias[0:1, :]
    normed, inverse = normalized(conv)
    normed_w[...] = normed
    inv_w[...] = jnp.broadcast_to(inverse, inv_w.shape)
    act, slope = gelu_parts(normed * norm_gain[0:1, :] + norm_bias[0:1, :])
    slope_w[...] = slope * norm_gain[0:1, :]
    act = act.astype(BF16)
    even, odd = act[:frames], act[frames:]
    act_t[0:channels, :] = even.T
    act_t[channels:, :] = odd.T
    (conv_narrow,) = loads.take(1)
    conv = dot(even, conv_narrow[0:channels, :]) + dot(odd, conv_narrow[channels:, :]) + conv_bias[1:2, :]
    normed, inverse = normalized(conv)
    normed_n[...] = normed
    inv_n[...] = jnp.broadcast_to(inverse, inv_n.shape)
    act, slope = gelu_parts(normed * norm_gain[1:2, :] + norm_bias[1:2, :])
    slope_n[...] = slope * norm_gain[1:2, :]
    unit, inverse = normalized(act.astype(BF16).astype(F32))
    unit_out[...] = unit
    row_inv[...] = jnp.broadcast_to(inverse, row_inv.shape)
    proj_gain, proj_bias, proj_weight = loads.take(3)
    normed_in = (unit * proj_gain[...]).astype(BF16)
    projected = dot(normed_in, proj_weight[...]) + proj_bias[...]
    proj_t[...] = projected.astype(BF16).T


def owned_rows(left, owner, outer):
    part = left.shape[0] // (2 * outer)
    return [left.at[pl.ds(pl.multiple_of((2 * block + owner) * part, part), part), :] for block in range(outer)]


def weight_grad(loads, grads, factor, target):
    outer, inner = target.shape[0], target.shape[1]
    row = 0
    for grad in grads:
        for block, left in enumerate(loads.take(outer)):
            value = (dot(left[...], grad) * factor).astype(BF16)
            each = left.shape[0] // inner
            for k in range(inner):
                target[block, k, row : row + each, :] = value[k * each : (k + 1) * each]
        row += each


def backward_kernel(factor, *refs):
    tm = lax.axis_size("tm")
    count = 13 + tm
    sources, (send, grad_conv, grad_low), rest = refs[:count], refs[count : count + 3], refs[count + 3 :]
    *held, grad_t, sems = rest
    outer = send.shape[0]
    own = lax.axis_index("tm")
    rows = sources[1].shape[0]
    places = [grad_t.at[pl.ds(pl.multiple_of((own ^ k) * rows, rows), rows), :] for k in range(tm)]
    other = 1 - lax.axis_index("dp") % 2
    lefts = [rows for left in sources[-2:] for rows in owned_rows(left, other, outer)]
    loads = Loads([*sources[:-2], *lefts], [held[0], *places, *held[1:]], sems)
    proj_weight, *_, proj_gain = loads.take(2 + tm)
    grad_unit = dot(proj_weight[...], grad_t[...]).T * proj_gain[...]
    unit_in, row_inv = loads.take(2)
    frames, channels = unit_in.shape
    unit = unit_in[...]
    grad_last = row_inv[:, 0:1] * (grad_unit - row_mean(grad_unit) - unit * row_mean(grad_unit * unit))
    normed_n, slope_n, inv_n, conv_narrow = loads.take(4)
    grad_normed = grad_last.astype(BF16).astype(F32) * slope_n[...]
    normed = normed_n[...]
    grad_narrow = (
        inv_n[:, 0:1] * (grad_normed - row_mean(grad_normed) - normed * row_mean(grad_normed * normed))
    ).astype(BF16)
    grad_low[...] = grad_narrow
    normed_w, slope_w, inv_w = loads.take(3)
    for parity in range(2):
        at = pl.ds(parity * frames, frames)
        grad_first = dot_nt(grad_narrow, conv_narrow[parity * channels : (parity + 1) * channels, :]).astype(BF16)
        grad_normed = grad_first.astype(F32) * slope_w[at, :]
        normed = normed_w[at, :]
        grad_conv[at, :] = (
            inv_w[at, 0:1] * (grad_normed - row_mean(grad_normed) - normed * row_mean(grad_normed * normed))
        ).astype(BF16)
    weight_grad(loads, (grad_conv[...], grad_narrow), factor, send)


def own_grad_kernel(factor, patch_t, act_t, conv_wide, grad_conv, grad_low, keep, tail, *rest):
    held, sems = rest[:-1], rest[-1]
    outer = keep.shape[0]
    core = lax.axis_index("dp") % 2
    lefts = [rows for left in (patch_t, act_t) for rows in owned_rows(left, core, outer)]
    last_tap = held[-1].shape[0]
    loads = Loads([*lefts, conv_wide.at[pl.ds(2 * last_tap, last_tap), :]], held, sems)
    grad_wide = grad_conv[...]
    weight_grad(loads, (grad_wide, grad_low[...]), factor, keep)
    (tap,) = loads.take(1)
    tail[...] = dot_nt(grad_wide[grad_wide.shape[0] - 8 :, :], tap[...])


def input_grad_kernel(grad_conv, conv_wide, out, first_rows, spread):
    frames = grad_conv.shape[0] // 2
    channels = grad_conv.shape[1]
    even, odd = grad_conv[:frames, :], grad_conv[frames:, :]
    taps = [conv_wide[tap * channels : (tap + 1) * channels, :] for tap in range(3)]
    shifted = pltpu.roll(dot_nt(odd, taps[2]), 1, axis=0)
    at_start = lax.broadcasted_iota(jnp.int32, (frames, 1), 0) == 0
    shifted = jnp.where(at_start, 0.0, shifted)
    put_rows(spread, 0, dot_nt(even, taps[0]) + shifted)
    put_rows(spread, 1, dot_nt(even, taps[1]))
    put_rows(spread, 2, dot_nt(even, taps[2]) + dot_nt(odd, taps[0]))
    put_rows(spread, 3, dot_nt(odd, taps[1]))
    for lane in range(channels // 128):
        out[:, lane * 128 : (lane + 1) * 128] = spread[lane].astype(BF16)
        first_rows[:, lane * 128 : (lane + 1) * 128] = spread[lane, 0:8, :]


def first_sum_kernel(keep, received, *outs):
    y = lax.axis_index("dp") // 2
    x = lax.axis_index("tm") % 2
    inner = keep.shape[1] // 2
    for flip, out in enumerate(outs):
        block = y ^ (flip // 2)
        lane = x ^ (flip % 2)
        for z in range(inner):
            at = 2 * z + lane
            out[z] = (keep[block, at].astype(F32) + received[block, at].astype(F32)).astype(BF16)


def second_sum_kernel(a, b, c, d, *outs):
    z = lax.axis_index("tm") // 2
    for flip, out in enumerate(outs):
        at = z ^ flip
        total = (a[at].astype(F32) + b[at].astype(F32)) + (c[at].astype(F32) + d[at].astype(F32))
        out[...] = total.astype(BF16)


def last_sum_kernel(wide_rows, a, b, c, d, incoming, first_rows, grad_in, wide, narrow, grad_out, rows_buf, sem):
    at_start = lax.broadcasted_iota(jnp.int32, (8, 1), 0) == 0
    rows_buf[...] = (first_rows[...] + jnp.where(at_start, incoming[7:8, :], 0.0)).astype(BF16)
    put = pltpu.make_async_copy(rows_buf, grad_out.at[pl.ds(0, 8), :], sem)
    put.start()
    total = (a[...].astype(F32) + b[...].astype(F32)) + (c[...].astype(F32) + d[...].astype(F32))
    rows, channels = total.shape
    pieces = channels // 128
    for p in range(pieces):
        lanes = total[:, p * 128 : (p + 1) * 128]
        wide[pl.ds(p, wide_rows, stride=pieces), :] = lanes[:wide_rows]
        narrow[pl.ds(p, rows - wide_rows, stride=pieces), :] = lanes[wide_rows:]
    put.wait()


def flipped(dy, dc, dz, dx):
    dp, tm = lax.axis_size("dp"), lax.axis_size("tm")
    change_dp, change_tm = 2 * dy + dc, 2 * dz + dx
    return [
        (p * tm + t, (p ^ change_dp) * tm + (t ^ change_tm)) for p in range(dp) for t in range(tm)
    ]


def swap(value, dy, dc, dz, dx):
    return lax.ppermute(value, ("dp", "tm"), flipped(dy, dc, dz, dx))


def shards(
    features,
    conv_wide,
    conv_narrow,
    conv_bias,
    norm_gain,
    norm_bias,
    proj_gain,
    proj_weight,
    proj_bias,
    upstream,
):
    dp, tm = lax.axis_size("dp"), lax.axis_size("tm")
    recs_local, length, channels = features.shape
    pairs, frames_total, depth = upstream.shape
    frames = frames_total // tm
    if not (dp == 4 and tm == 8 and recs_local == 1 and frames % 128 == 0 and pairs * tm == HEADS):
        return generic_shards(
            features,
            conv_wide,
            conv_narrow,
            conv_bias,
            norm_gain,
            norm_bias,
            proj_gain,
            proj_weight,
            proj_bias,
            upstream,
        )
    width = HEADS * depth
    factor = 1.0 / math.sqrt(recs_local * dp * frames_total)
    sems = [pltpu.SemaphoreType.DMA((tm,))]
    cuts = local(
        cut_kernel,
        [upstream.transpose(0, 2, 1)],
        [((pairs, depth, frames), BF16, False)] * tm,
        "cut",
        scratch=[pltpu.VMEM((tm, pairs, depth, frames), BF16)] + sems * 2,
        raw=(0,),
        raw_out=range(tm),
    )
    cuts = [cut.reshape(pairs * depth, frames) for cut in cuts]
    heads_in = {0: cuts[0]}
    for k in (6, 7, 4, 5, 2, 3, 1):
        heads_in[k] = swap(cuts[k], 0, 0, k // 2, k % 2)
    signal = features.reshape(length, channels)
    halo = passed_along(signal[:8], "tm", -1)
    wide_rows = 2 * frames
    spread = pltpu.VMEM((channels // 128, length, 128), F32)
    gain = proj_gain.reshape(1, channels)
    forward_in = [
        signal,
        halo,
        conv_bias,
        norm_gain,
        norm_bias,
        conv_wide,
        conv_narrow,
        gain,
        proj_bias.reshape(1, width),
        proj_weight,
    ]
    proj_t, *stored = local(
        forward_kernel,
        forward_in,
        [
            ((width, frames), BF16, False),
            ((3 * channels, wide_rows), BF16, False),
            ((2 * channels, frames), BF16, False),
            ((wide_rows, channels), F32, False),
            ((wide_rows, channels), F32, False),
            ((wide_rows, 128), F32, False),
            ((frames, channels), F32, False),
            ((frames, channels), F32, False),
            ((frames, 128), F32, False),
            ((frames, channels), F32, False),
            ((frames, 128), F32, False),
        ],
        "forward",
        limit=32,
        scratch=[pltpu.VMEM(x.shape, x.dtype) for x in forward_in]
        + [
            pltpu.SemaphoreType.DMA((len(forward_in),)),
            spread,
            pltpu.VMEM((wide_rows, 3 * channels), BF16),
        ],
        raw=range(len(forward_in)),
    )
    proj_t, heads_in[4] = lax.optimization_barrier((proj_t, heads_in[4]))
    heads = lax.all_to_all(
        proj_t.reshape(tm, pairs * depth, frames), "tm", split_axis=0, concat_axis=0, tiled=True
    )
    outer, inner = dp // 2, tm
    part_rows = 5 * channels // (dp * tm)
    part = ((outer, inner, part_rows, channels), BF16, True)
    patch_t, act_t, normed_w, slope_w, inv_w, normed_n, slope_n, inv_n, unit, row_inv = stored
    inputs = [
        proj_weight,
        *[heads_in[k] for k in range(tm)],
        gain,
        unit,
        row_inv,
        normed_n,
        slope_n,
        inv_n,
        conv_narrow,
        normed_w,
        slope_w,
        inv_w,
        patch_t,
        act_t,
    ]
    lefts = [
        pltpu.VMEM((x.shape[0] // (2 * outer), x.shape[1]), BF16)
        for x in (patch_t, act_t)
        for _ in range(outer)
    ]
    held = [pltpu.VMEM(x.shape, x.dtype) for x in inputs[:1] + inputs[tm + 1 : -2]] + lefts
    grad_buf = pltpu.VMEM((width, frames), BF16)
    send, grad_conv, grad_low = local(
        lambda *refs: backward_kernel(factor, *refs),
        inputs,
        [part, ((wide_rows, channels), BF16, True), ((frames, channels), BF16, True)],
        "backward",
        limit=24,
        scratch=held + [grad_buf, pltpu.SemaphoreType.DMA((len(held) + tm,))],
        raw=range(len(inputs)),
    )
    received = swap(send, 0, 1, 0, 0)
    held = lefts + [pltpu.VMEM((channels, channels), BF16)]
    keep, tail = local(
        lambda *refs: own_grad_kernel(factor, *refs),
        [patch_t, act_t, conv_wide, grad_conv, grad_low],
        [part, ((8, channels), F32, True)],
        "own_grad",
        scratch=held + [pltpu.SemaphoreType.DMA((len(held),))],
        raw=(0, 1, 2),
    )
    plane = ((tm // 2, part_rows, channels), BF16, True)
    own, *outgoing = local(first_sum_kernel, [keep, received], [plane] * 4, "first_sum")
    arrived = [swap(value, k // 2, 0, 0, k % 2) for k, value in enumerate(outgoing, 1)]
    tail, grad_conv, own = lax.optimization_barrier((tail, grad_conv, own))
    incoming = passed_along(tail, "tm", 1)
    feature_grad, first_rows = local(
        input_grad_kernel,
        [grad_conv, conv_wide],
        [((length, channels), BF16, False), ((8, channels), F32, True)],
        "input_grad",
        scratch=[spread],
    )
    piece = ((part_rows, channels), BF16, True)
    (attn_t,) = local(
        join_kernel,
        [heads.reshape(tm, pairs, depth, frames)],
        [((pairs, depth, frames_total), BF16, False)],
        "join",
        scratch=sems,
        raw_out=(0,),
    )
    attn_t, first_rows, own = lax.optimization_barrier((attn_t, first_rows, own))
    own, *outgoing = local(second_sum_kernel, [own, *arrived], [piece] * 4, "second_sum")
    arrived = [swap(value, 0, 0, k, 0) for k, value in enumerate(outgoing, 1)]
    own_wide = 3 * channels // (dp * tm)
    wide, narrow, feature_grad = local(
        lambda *refs: last_sum_kernel(own_wide, *refs),
        [own, *arrived, incoming, first_rows, feature_grad],
        [
            ((own_wide * channels // 128, 128), F32, False),
            (((part_rows - own_wide) * channels // 128, 128), F32, False),
            ((length, channels), BF16, False),
        ],
        "last_sum",
        scratch=[pltpu.VMEM((8, channels), BF16), pltpu.SemaphoreType.DMA(())],
        raw=(6,),
        raw_out=(2,),
        aliases={6: 2},
    )
    return (
        attn_t.transpose(0, 2, 1),
        feature_grad.reshape(recs_local, length, channels),
        wide.reshape(-1),
        narrow.reshape(-1),
    )


def solution(mesh):
    in_specs = (
        P("dp", "tm", None),
        P(),
        P(),
        P(),
        P(),
        P(),
        P(),
        P(),
        P(),
        P(("dp", "tm"), None, None),
    )
    out_specs = (P(("dp", "tm"), None, None), P("dp", "tm", None), P(("dp", "tm")), P(("dp", "tm")))
    return jax.shard_map(shards, mesh=mesh, in_specs=in_specs, out_specs=out_specs, check_vma=False)
```

```python
import math

import jax
import jax.numpy as jnp
from jax import lax
from jax.experimental import pallas as pl
from jax.experimental.pallas import tpu as pltpu
from jax.sharding import PartitionSpec as P

HEADS = 16
HEAD_DIM = 120


EPSILON = 1e-05
SQRT_HALF = 0.7071067811865476
INV_ROOT_TAU = 0.3989422804014327


def passed_along(value, axis, steps):
    count = lax.axis_size(axis)
    leading, last = (max(0, -steps), min(count, count - steps))
    return lax.ppermute(value, axis, [(source, source + steps) for source in range(leading, last)])


def gelu_exact(values):
    return 0.5 * values * (1.0 + lax.erf(values * SQRT_HALF))


def gelu_slope(values):
    cumulative = 0.5 * (1.0 + lax.erf(values * SQRT_HALF))
    density = jnp.exp(-0.5 * values * values) * INV_ROOT_TAU
    return cumulative + values * density


def wide_patches(signal, first_next):
    recs_local, length, channels = signal.shape
    paired = signal.reshape(recs_local, length // 2, 2 * channels)
    following = jnp.concatenate([paired[:, 1:, :channels], first_next], axis=1)
    return jnp.concatenate([paired, following], axis=2)


def narrow_patches(signal):
    recs_local, length, channels = signal.shape
    return signal.reshape(recs_local, length // 2, 2 * channels)


def conv_forward(patches, weight, bias_conv, gain_row, bias_row):
    recs_local, out_rows, patch_width = patches.shape
    conv_out = jnp.dot(
        patches.reshape(recs_local * out_rows, patch_width),
        weight,
        preferred_element_type=jnp.float32,
    )
    conv_out = conv_out.reshape(recs_local, out_rows, weight.shape[1]) + bias_conv
    center = jnp.mean(conv_out, axis=2, keepdims=True)
    centered = conv_out - center
    inverse = lax.rsqrt(jnp.mean(centered * centered, axis=2, keepdims=True) + EPSILON)
    normed = centered * inverse
    preact = normed * gain_row + bias_row
    activated = gelu_exact(preact).astype(jnp.bfloat16)
    return (activated, (patches, normed, preact, inverse))


def conv_backward(grad_act, weight, gain_row, stored):
    patches, normed, preact, inverse = stored
    recs_local, out_rows, patch_width = patches.shape
    grad_normed = grad_act.astype(jnp.float32) * gelu_slope(preact) * gain_row
    avg_grad = jnp.mean(grad_normed, axis=2, keepdims=True)
    avg_cross = jnp.mean(grad_normed * normed, axis=2, keepdims=True)
    grad_conv = (inverse * (grad_normed - avg_grad - normed * avg_cross)).astype(jnp.bfloat16)
    flat_patches = patches.reshape(recs_local * out_rows, patch_width)
    flat_grad = grad_conv.reshape(recs_local * out_rows, weight.shape[1])
    weight_grad = lax.dot_general(
        flat_patches, flat_grad, (((0,), (0,)), ((), ())), preferred_element_type=jnp.float32
    )
    grad_patch = lax.dot_general(
        flat_grad, weight, (((1,), (1,)), ((), ())), preferred_element_type=jnp.float32
    )
    return (weight_grad, grad_patch.reshape(recs_local, out_rows, patch_width))


def wide_input_grad(grad_patch, channels):
    recs_local, out_rows, patch_width = grad_patch.shape
    tail = grad_patch[:, :, 2 * channels :]
    incoming = passed_along(tail[:, -1:], "tm", 1)
    shifted = jnp.concatenate([incoming, tail[:, :-1]], axis=1)
    first_half = grad_patch[:, :, :channels] + shifted
    combined = jnp.concatenate([first_half, grad_patch[:, :, channels : 2 * channels]], axis=2)
    return combined.reshape(recs_local, 2 * out_rows, channels).astype(jnp.bfloat16)


def narrow_input_grad(grad_patch, channels):
    recs_local, out_rows, patch_width = grad_patch.shape
    return grad_patch.reshape(recs_local, 2 * out_rows, channels).astype(jnp.bfloat16)


def share_grad(weight_grad, factor):
    flat = (weight_grad * factor).reshape(-1)
    result = lax.psum_scatter(flat, ("dp", "tm"), scatter_dimension=0, tiled=True)
    return result


def generic_shards(
    features,
    conv_wide,
    conv_narrow,
    conv_bias,
    norm_gain,
    norm_bias,
    proj_gain,
    proj_weight,
    proj_bias,
    upstream,
):
    recs_local, length, channels = features.shape
    tm_count = lax.axis_size("tm")
    frames_total = upstream.shape[1]
    frames_local = frames_total // tm_count
    factor = 1.0 / math.sqrt(recs_local * lax.axis_size("dp") * frames_total)
    grad_frames = lax.all_to_all(upstream, "tm", split_axis=1, concat_axis=0, tiled=True)
    first_next = passed_along(features[:, :1], "tm", -1)
    act_wide, stored_wide = conv_forward(
        wide_patches(features, first_next), conv_wide, conv_bias[0], norm_gain[0], norm_bias[0]
    )
    act_narrow, stored_narrow = conv_forward(
        narrow_patches(act_wide), conv_narrow, conv_bias[1], norm_gain[1], norm_bias[1]
    )
    widened = act_narrow.astype(jnp.float32)
    centered = widened - jnp.mean(widened, axis=2, keepdims=True)
    row_inverse = lax.rsqrt(jnp.mean(centered * centered, axis=2, keepdims=True) + EPSILON)
    unit_rows = centered * row_inverse
    normed_in = (unit_rows * proj_gain).astype(jnp.bfloat16)
    weight_heads = proj_weight.reshape(channels, HEADS, HEAD_DIM)
    projected = jnp.einsum(
        "rfc,chd->rhfd", normed_in, weight_heads, preferred_element_type=jnp.float32
    ) + proj_bias.reshape(HEADS, 1, HEAD_DIM)
    heads_local = projected.astype(jnp.bfloat16).reshape(recs_local * HEADS, frames_local, HEAD_DIM)
    attn_input = lax.all_to_all(heads_local, "tm", split_axis=0, concat_axis=1, tiled=True)
    grad_heads = grad_frames.reshape(recs_local, HEADS, frames_local, HEAD_DIM)
    grad_unit = (
        jnp.einsum("rhfd,chd->rfc", grad_heads, weight_heads, preferred_element_type=jnp.float32)
        * proj_gain
    )
    grad_last = (
        row_inverse
        * (
            grad_unit
            - jnp.mean(grad_unit, axis=2, keepdims=True)
            - unit_rows * jnp.mean(grad_unit * unit_rows, axis=2, keepdims=True)
        )
    ).astype(jnp.bfloat16)
    weight_narrow, patch_narrow = conv_backward(grad_last, conv_narrow, norm_gain[1], stored_narrow)
    grad_conv_narrow = share_grad(weight_narrow, factor)
    grad_first = narrow_input_grad(patch_narrow, channels)
    weight_wide, patch_wide = conv_backward(grad_first, conv_wide, norm_gain[0], stored_wide)
    grad_conv_wide = share_grad(weight_wide, factor)
    feature_grad = wide_input_grad(patch_wide, channels)
    return (attn_input, feature_grad, grad_conv_wide, grad_conv_narrow)


F32 = jnp.float32
ORDER = (0, 6, 7, 4, 5, 2, 3, 1)
BF16 = jnp.bfloat16
NT = (((1,), (1,)), ((), ()))


def dot(a, b):
    return jnp.dot(a, b, preferred_element_type=F32)


def dot_nt(a, b):
    return lax.dot_general(a, b, NT, preferred_element_type=F32)


def row_mean(values):
    return jnp.mean(values, axis=1, keepdims=True)


def normalized(values):
    centered = values - row_mean(values)
    inverse = lax.rsqrt(row_mean(centered * centered) + EPSILON)
    return centered * inverse, inverse


def gelu_parts(preact):
    cumulative = 0.5 * (1.0 + lax.erf(preact * SQRT_HALF))
    slope = cumulative + preact * (jnp.exp(-0.5 * preact * preact) * INV_ROOT_TAU)
    return preact * cumulative, slope


def local(kernel, operands, outs, name, limit=16, scratch=(), raw=(), raw_out=(), free=(), aliases=None, cost=1000):
    out_shape, out_specs = [], []
    for number, (shape, dtype, stays) in enumerate(outs):
        out_shape.append((pltpu.VMEM if stays else pltpu.HBM)(shape, dtype))
        out_specs.append(pl.BlockSpec(memory_space=pltpu.HBM if number in raw_out else pltpu.VMEM))
    held = [
        x if k in free else pltpu.with_memory_space_constraint(x, pltpu.HBM if k in raw else pltpu.VMEM)
        for k, x in enumerate(operands)
    ]
    return pl.pallas_call(
        kernel,
        out_shape=out_shape,
        in_specs=[
            pl.BlockSpec(memory_space=pl.ANY if k in free else pltpu.HBM if k in raw else pltpu.VMEM)
            for k in range(len(operands))
        ],
        out_specs=out_specs,
        scratch_shapes=list(scratch),
        input_output_aliases=aliases or {},
        compiler_params=pltpu.CompilerParams(vmem_limit_bytes=limit << 20),
        cost_estimate=pl.CostEstimate(flops=cost, bytes_accessed=0, transcendentals=0),
        name=name,
    )(*held)


def run_copies(pairs, sems):
    copies = [pltpu.make_async_copy(src, dst, sems.at[k]) for k, (src, dst) in enumerate(pairs)]
    for copy in copies:
        copy.start()
    for copy in copies:
        copy.wait()


def first_cut_kernel(flips, whole, signal, *refs):
    *parts, first_rows, sems = refs
    width = parts[0].shape[2]
    own = lax.axis_index("tm")
    starts = [pl.multiple_of((own ^ flip) * width, width) for flip in flips]
    pairs = [(whole.at[:, :, pl.ds(start, width)], part) for start, part in zip(starts, parts)]
    run_copies([*pairs, (signal.at[pl.ds(0, 8), :], first_rows)], sems)


def rest_cut_kernel(flips, whole, *refs):
    *parts, held, sems, out_sems = refs
    width = held.shape[3]
    own = lax.axis_index("tm")
    reads, writes = [], []
    for k, flip in enumerate(flips):
        start = pl.multiple_of((own ^ flip) * width, width)
        reads.append(pltpu.make_async_copy(whole.at[:, :, pl.ds(start, width)], held.at[k], sems.at[k]))
        writes.append(pltpu.make_async_copy(held.at[k], parts[k], out_sems.at[k]))
    for read in reads:
        read.start()
    for read, write in zip(reads, writes):
        read.wait()
        write.start()
    for write in writes:
        write.wait()


def join_kernel(parts, whole, sems):
    width = parts.shape[3]
    run_copies([(parts.at[k], whole.at[:, :, pl.ds(k * width, width)]) for k in range(parts.shape[0])], sems)


class Loads:
    def __init__(self, sources, held, sems):
        self.pairs = [
            (pltpu.make_async_copy(src, buf, sems.at[k]), buf) for k, (src, buf) in enumerate(zip(sources, held))
        ]
        for read, _ in self.pairs:
            read.start()

    def take(self, count):
        taken, self.pairs = self.pairs[:count], self.pairs[count:]
        for read, _ in taken:
            read.wait()
        return [buf for _, buf in taken]


def spread_rows(spread, first, count):
    lanes = [spread[lane, pl.ds(first, count, stride=4), :] for lane in range(spread.shape[0])]
    return jnp.concatenate(lanes, axis=1)


def put_rows(spread, first, value):
    for lane in range(spread.shape[0]):
        spread[lane, pl.ds(first, value.shape[0], stride=4), :] = value[:, lane * 128 : (lane + 1) * 128]


def forward_kernel(*refs):
    sources, outs, rest = refs[:10], refs[10:21], refs[21:]
    *held, sems, out_sems, spread, patches = rest
    held, bufs = held[:10], held[10:]
    writes = []

    def put(number):
        write = pltpu.make_async_copy(bufs[number], outs[number], out_sems.at[number])
        write.start()
        writes.append(write)

    (
        proj_t,
        patch_t,
        act_t,
        normed_w,
        slope_w,
        inv_w,
        normed_n,
        slope_n,
        inv_n,
        unit_out,
        row_inv,
    ) = bufs
    loads = Loads(sources, held, sems)
    feat, halo, conv_bias, norm_gain, norm_bias = loads.take(5)
    frames = feat.shape[0] // 4
    channels = feat.shape[1]
    for lane in range(channels // 128):
        spread[lane] = feat[:, lane * 128 : (lane + 1) * 128].astype(F32)
    rows = [spread_rows(spread, j, frames) for j in range(4)]
    following = pltpu.roll(rows[0], frames - 1, axis=0)
    at_end = lax.broadcasted_iota(jnp.int32, (frames, 1), 0) == frames - 1
    rows.append(jnp.where(at_end, halo[0:1, :].astype(F32), following))
    rows = [row.astype(BF16) for row in rows]
    for parity in range(2):
        for tap in range(3):
            piece = rows[2 * parity + tap]
            patches[parity * frames : (parity + 1) * frames, tap * channels : (tap + 1) * channels] = piece
            patch_t[tap * channels : (tap + 1) * channels, parity * frames : (parity + 1) * frames] = piece.T
    put(1)
    (conv_wide,) = loads.take(1)
    conv = dot(patches[...], conv_wide[...]) + conv_bias[0:1, :]
    normed, inverse = normalized(conv)
    normed_w[...] = normed
    inv_w[...] = jnp.broadcast_to(inverse, inv_w.shape)
    put(3)
    put(5)
    act, slope = gelu_parts(normed * norm_gain[0:1, :] + norm_bias[0:1, :])
    slope_w[...] = slope * norm_gain[0:1, :]
    put(4)
    act = act.astype(BF16)
    even, odd = act[:frames], act[frames:]
    act_t[0:channels, :] = even.T
    act_t[channels:, :] = odd.T
    put(2)
    (conv_narrow,) = loads.take(1)
    conv = dot(even, conv_narrow[0:channels, :]) + dot(odd, conv_narrow[channels:, :]) + conv_bias[1:2, :]
    normed, inverse = normalized(conv)
    normed_n[...] = normed
    inv_n[...] = jnp.broadcast_to(inverse, inv_n.shape)
    put(6)
    put(8)
    act, slope = gelu_parts(normed * norm_gain[1:2, :] + norm_bias[1:2, :])
    slope_n[...] = slope * norm_gain[1:2, :]
    put(7)
    unit, inverse = normalized(act.astype(BF16).astype(F32))
    unit_out[...] = unit
    row_inv[...] = jnp.broadcast_to(inverse, row_inv.shape)
    put(9)
    put(10)
    proj_gain, proj_bias, proj_weight = loads.take(3)
    normed_in = (unit * proj_gain[...]).astype(BF16)
    bias = jnp.concatenate([proj_bias[k : k + 1, :] for k in range(proj_bias.shape[0])], axis=1)
    projected = dot(normed_in, proj_weight[...]) + bias
    proj_t[...] = projected.astype(BF16).T
    put(0)
    for write in writes:
        write.wait()


def owned_rows(left, owner, outer):
    part = left.shape[0] // (2 * outer)
    return [left.at[pl.ds(pl.multiple_of((2 * block + owner) * part, part), part), :] for block in range(outer)]


def weight_grad(loads, grads, factor, target):
    outer, inner = target.shape[0], target.shape[1]
    row = 0
    for grad in grads:
        for block, left in enumerate(loads.take(outer)):
            value = (dot(left[...], grad) * factor).astype(BF16)
            each = left.shape[0] // inner
            for k in range(inner):
                target[block, k, row : row + each, :] = value[k * each : (k + 1) * each]
        row += each


def backward_kernel(factor, *refs):
    tm = lax.axis_size("tm")
    count = 13 + tm
    sources, (send, grad_conv, grad_low), rest = refs[:count], refs[count : count + 3], refs[count + 3 :]
    *held, grad_t, sems = rest
    outer = send.shape[0]
    own = lax.axis_index("tm")
    rows = sources[1].shape[0]
    places = [grad_t.at[pl.ds(pl.multiple_of((own ^ k) * rows, rows), rows), :] for k in ORDER]
    other = 1 - lax.axis_index("dp") % 2
    lefts = [rows for left in sources[-2:] for rows in owned_rows(left, other, outer)]
    loads = Loads([*sources[:-2], *lefts], [held[0], *places, *held[1:]], sems)
    proj_weight, *_, proj_gain = loads.take(2 + tm)
    grad_unit = dot(proj_weight[...], grad_t[...]).T * proj_gain[...]
    unit_in, row_inv = loads.take(2)
    frames, channels = unit_in.shape
    unit = unit_in[...]
    grad_last = row_inv[:, 0:1] * (grad_unit - row_mean(grad_unit) - unit * row_mean(grad_unit * unit))
    normed_n, slope_n, inv_n, conv_narrow = loads.take(4)
    grad_normed = grad_last.astype(BF16).astype(F32) * slope_n[...]
    normed = normed_n[...]
    grad_narrow = (
        inv_n[:, 0:1] * (grad_normed - row_mean(grad_normed) - normed * row_mean(grad_normed * normed))
    ).astype(BF16)
    grad_low[...] = grad_narrow
    normed_w, slope_w, inv_w = loads.take(3)
    for parity in range(2):
        at = pl.ds(parity * frames, frames)
        grad_first = dot_nt(grad_narrow, conv_narrow[parity * channels : (parity + 1) * channels, :]).astype(BF16)
        grad_normed = grad_first.astype(F32) * slope_w[at, :]
        normed = normed_w[at, :]
        grad_conv[at, :] = (
            inv_w[at, 0:1] * (grad_normed - row_mean(grad_normed) - normed * row_mean(grad_normed * normed))
        ).astype(BF16)
    weight_grad(loads, (grad_conv[...], grad_narrow), factor, send)


def own_grad_kernel(factor, patch_t, act_t, conv_wide, grad_conv, grad_low, keep, tail, *rest):
    held, sems = rest[:-1], rest[-1]
    outer = keep.shape[0]
    core = lax.axis_index("dp") % 2
    lefts = [rows for left in (patch_t, act_t) for rows in owned_rows(left, core, outer)]
    last_tap = held[-1].shape[0]
    loads = Loads([*lefts, conv_wide.at[pl.ds(2 * last_tap, last_tap), :]], held, sems)
    grad_wide = grad_conv[...]
    weight_grad(loads, (grad_wide, grad_low[...]), factor, keep)
    (tap,) = loads.take(1)
    tail[...] = dot_nt(grad_wide[grad_wide.shape[0] - 8 :, :], tap[...])


def input_grad_kernel(grad_conv, conv_wide, out, first_rows, spread):
    frames = grad_conv.shape[0] // 2
    channels = grad_conv.shape[1]
    even, odd = grad_conv[:frames, :], grad_conv[frames:, :]
    taps = [conv_wide[tap * channels : (tap + 1) * channels, :] for tap in range(3)]
    shifted = pltpu.roll(dot_nt(odd, taps[2]), 1, axis=0)
    at_start = lax.broadcasted_iota(jnp.int32, (frames, 1), 0) == 0
    shifted = jnp.where(at_start, 0.0, shifted)
    put_rows(spread, 0, dot_nt(even, taps[0]) + shifted)
    put_rows(spread, 1, dot_nt(even, taps[1]))
    put_rows(spread, 2, dot_nt(even, taps[2]) + dot_nt(odd, taps[0]))
    put_rows(spread, 3, dot_nt(odd, taps[1]))
    for lane in range(channels // 128):
        out[:, lane * 128 : (lane + 1) * 128] = spread[lane].astype(BF16)
        first_rows[:, lane * 128 : (lane + 1) * 128] = spread[lane, 0:8, :]


def first_sum_kernel(keep, received, *outs):
    y = lax.axis_index("dp") // 2
    x = lax.axis_index("tm") % 2
    inner = keep.shape[1] // 2
    for flip, out in enumerate(outs):
        block = y ^ (flip // 2)
        lane = x ^ (flip % 2)
        for z in range(inner):
            at = 2 * z + lane
            out[z] = (keep[block, at].astype(F32) + received[block, at].astype(F32)).astype(BF16)


def second_sum_kernel(a, b, c, d, *outs):
    z = lax.axis_index("tm") // 2
    for flip, out in enumerate(outs):
        at = z ^ flip
        total = (a[at].astype(F32) + b[at].astype(F32)) + (c[at].astype(F32) + d[at].astype(F32))
        out[...] = total.astype(BF16)


def last_sum_kernel(wide_rows, a, b, c, d, incoming, first_rows, grad_in, wide, narrow, grad_out, rows_buf, sem):
    at_start = lax.broadcasted_iota(jnp.int32, (8, 1), 0) == 0
    rows_buf[...] = (first_rows[...] + jnp.where(at_start, incoming[7:8, :], 0.0)).astype(BF16)
    put = pltpu.make_async_copy(rows_buf, grad_out.at[pl.ds(0, 8), :], sem)
    put.start()
    total = (a[...].astype(F32) + b[...].astype(F32)) + (c[...].astype(F32) + d[...].astype(F32))
    rows, channels = total.shape
    pieces = channels // 128
    for p in range(pieces):
        lanes = total[:, p * 128 : (p + 1) * 128]
        wide[pl.ds(p, wide_rows, stride=pieces), :] = lanes[:wide_rows]
        narrow[pl.ds(p, rows - wide_rows, stride=pieces), :] = lanes[wide_rows:]
    put.wait()


def flipped(dy, dc, dz, dx):
    dp, tm = lax.axis_size("dp"), lax.axis_size("tm")
    change_dp, change_tm = 2 * dy + dc, 2 * dz + dx
    return [
        (p * tm + t, (p ^ change_dp) * tm + (t ^ change_tm)) for p in range(dp) for t in range(tm)
    ]


def swap(value, dy, dc, dz, dx):
    return lax.ppermute(value, ("dp", "tm"), flipped(dy, dc, dz, dx))


def shards(
    features,
    conv_wide,
    conv_narrow,
    conv_bias,
    norm_gain,
    norm_bias,
    proj_gain,
    proj_weight,
    proj_bias,
    upstream,
):
    dp, tm = lax.axis_size("dp"), lax.axis_size("tm")
    recs_local, length, channels = features.shape
    pairs, frames_total, depth = upstream.shape
    frames = frames_total // tm
    if not (dp == 4 and tm == 8 and recs_local == 1 and frames % 128 == 0 and HEADS * depth % 128 == 0 and pairs * tm == HEADS):
        return generic_shards(
            features,
            conv_wide,
            conv_narrow,
            conv_bias,
            norm_gain,
            norm_bias,
            proj_gain,
            proj_weight,
            proj_bias,
            upstream,
        )
    width = HEADS * depth
    factor = 1.0 / math.sqrt(recs_local * dp * frames_total)
    sems = [pltpu.SemaphoreType.DMA((tm,))]
    signal = features.reshape(length, channels)
    frames_cut = (pairs, depth, frames)
    early = (1, 6)
    late = [k for k in range(tm) if k not in early]
    *cuts, first_rows = local(
        lambda *refs: first_cut_kernel(early, *refs),
        [upstream.transpose(0, 2, 1), signal],
        [(frames_cut, BF16, True)] * len(early) + [((8, channels), BF16, True)],
        "cut",
        scratch=[pltpu.SemaphoreType.DMA((len(early) + 1,))],
        raw=(0, 1),
    )
    cuts += local(
        lambda *refs: rest_cut_kernel(late, *refs),
        [upstream.transpose(0, 2, 1)],
        [(frames_cut, BF16, False)] * len(late),
        "rest_cut",
        scratch=[pltpu.VMEM((len(late), *frames_cut), BF16)] + [pltpu.SemaphoreType.DMA((len(late),))] * 2,
        raw=(0,),
        raw_out=range(len(late)),
    )
    cuts = {k: cut.reshape(pairs * depth, frames) for k, cut in zip([*early, *late], cuts)}
    heads_in = {0: cuts[0]}
    for k in ORDER[1:]:
        heads_in[k] = swap(cuts[k], 0, 0, k // 2, k % 2)
    halo = passed_along(first_rows, "tm", -1)
    wide_rows = 2 * frames
    spread = pltpu.VMEM((channels // 128, length, 128), F32)
    gain = proj_gain.reshape(1, channels)
    forward_in = [
        signal,
        halo,
        conv_bias,
        norm_gain,
        norm_bias,
        conv_wide,
        conv_narrow,
        gain,
        proj_bias.reshape(width // 128, 128),
        proj_weight,
    ]
    forward_out = [
        ((width, frames), BF16, False),
        ((3 * channels, wide_rows), BF16, False),
        ((2 * channels, frames), BF16, False),
        ((wide_rows, channels), F32, False),
        ((wide_rows, channels), F32, False),
        ((wide_rows, 128), F32, False),
        ((frames, channels), F32, False),
        ((frames, channels), F32, False),
        ((frames, 128), F32, False),
        ((frames, channels), F32, False),
        ((frames, 128), F32, False),
    ]
    proj_t, *stored = local(
        forward_kernel,
        forward_in,
        forward_out,
        "forward",
        limit=40,
        scratch=[pltpu.VMEM(x.shape, x.dtype) for x in forward_in]
        + [pltpu.VMEM(shape, dtype) for shape, dtype, _ in forward_out]
        + [
            pltpu.SemaphoreType.DMA((len(forward_in),)),
            pltpu.SemaphoreType.DMA((len(forward_out),)),
            spread,
            pltpu.VMEM((wide_rows, 3 * channels), BF16),
        ],
        raw=range(len(forward_in)),
        raw_out=range(len(forward_out)),
    )
    proj_t, heads_in[1] = lax.optimization_barrier((proj_t, heads_in[1]))
    heads = lax.all_to_all(
        proj_t.reshape(tm, pairs * depth, frames), "tm", split_axis=0, concat_axis=0, tiled=True
    )
    outer, inner = dp // 2, tm
    part_rows = 5 * channels // (dp * tm)
    part = ((outer, inner, part_rows, channels), BF16, True)
    patch_t, act_t, normed_w, slope_w, inv_w, normed_n, slope_n, inv_n, unit, row_inv = stored
    inputs = [
        proj_weight,
        *[heads_in[k] for k in ORDER],
        gain,
        unit,
        row_inv,
        normed_n,
        slope_n,
        inv_n,
        conv_narrow,
        normed_w,
        slope_w,
        inv_w,
        patch_t,
        act_t,
    ]
    lefts = [
        pltpu.VMEM((x.shape[0] // (2 * outer), x.shape[1]), BF16)
        for x in (patch_t, act_t)
        for _ in range(outer)
    ]
    held = [pltpu.VMEM(x.shape, x.dtype) for x in inputs[:1] + inputs[tm + 1 : -2]] + lefts
    grad_buf = pltpu.VMEM((width, frames), BF16)
    send, grad_conv, grad_low = local(
        lambda *refs: backward_kernel(factor, *refs),
        inputs,
        [part, ((wide_rows, channels), BF16, True), ((frames, channels), BF16, True)],
        "backward",
        limit=24,
        scratch=held + [grad_buf, pltpu.SemaphoreType.DMA((len(held) + tm,))],
        raw=range(len(inputs)),
        free=range(1, tm + 1),
    )
    received = swap(send, 0, 1, 0, 0)
    held = lefts + [pltpu.VMEM((channels, channels), BF16)]
    keep, tail = local(
        lambda *refs: own_grad_kernel(factor, *refs),
        [patch_t, act_t, conv_wide, grad_conv, grad_low],
        [part, ((8, channels), F32, True)],
        "own_grad",
        scratch=held + [pltpu.SemaphoreType.DMA((len(held),))],
        raw=(0, 1, 2),
    )
    plane = ((tm // 2, part_rows, channels), BF16, True)
    own, *outgoing = local(first_sum_kernel, [keep, received], [plane] * 4, "first_sum")
    arrived = [swap(outgoing[k - 1], k // 2, 0, 0, k % 2) for k in (3, 1, 2)]
    tail, grad_conv, own = lax.optimization_barrier((tail, grad_conv, own))
    incoming = passed_along(tail, "tm", 1)
    feature_grad, first_rows = local(
        input_grad_kernel,
        [grad_conv, conv_wide],
        [((length, channels), BF16, False), ((8, channels), F32, True)],
        "input_grad",
        scratch=[spread],
    )
    piece = ((part_rows, channels), BF16, True)
    (attn_t,) = local(
        join_kernel,
        [heads.reshape(tm, pairs, depth, frames)],
        [((pairs, depth, frames_total), BF16, False)],
        "join",
        scratch=sems,
        raw_out=(0,),
    )
    attn_t, first_rows, incoming, own = lax.optimization_barrier((attn_t, first_rows, incoming, own))
    own, *outgoing = local(second_sum_kernel, [own, *arrived], [piece] * 4, "second_sum")
    arrived = [swap(outgoing[k - 1], 0, 0, k, 0) for k in (2, 3, 1)]
    own_wide = 3 * channels // (dp * tm)
    wide, narrow, feature_grad = local(
        lambda *refs: last_sum_kernel(own_wide, *refs),
        [own, *arrived, incoming, first_rows, feature_grad],
        [
            ((own_wide * channels // 128, 128), F32, False),
            (((part_rows - own_wide) * channels // 128, 128), F32, False),
            ((length, channels), BF16, False),
        ],
        "last_sum",
        scratch=[pltpu.VMEM((8, channels), BF16), pltpu.SemaphoreType.DMA(())],
        raw=(6,),
        raw_out=(2,),
        aliases={6: 2},
    )
    return (
        attn_t.transpose(0, 2, 1),
        feature_grad.reshape(recs_local, length, channels),
        wide.reshape(-1),
        narrow.reshape(-1),
    )


def solution(mesh):
    in_specs = (
        P("dp", "tm", None),
        P(),
        P(),
        P(),
        P(),
        P(),
        P(),
        P(),
        P(),
        P(("dp", "tm"), None, None),
    )
    out_specs = (P(("dp", "tm"), None, None), P("dp", "tm", None), P(("dp", "tm")), P(("dp", "tm")))
    return jax.shard_map(shards, mesh=mesh, in_specs=in_specs, out_specs=out_specs, check_vma=False)
```

```python
import math

import jax
import jax.numpy as jnp
from jax import lax
from jax.experimental import pallas as pl
from jax.experimental.pallas import tpu as pltpu
from jax.sharding import PartitionSpec as P

HEADS = 16
HEAD_DIM = 120


EPSILON = 1e-05
SQRT_HALF = 0.7071067811865476
INV_ROOT_TAU = 0.3989422804014327


def passed_along(value, axis, steps):
    count = lax.axis_size(axis)
    leading, last = (max(0, -steps), min(count, count - steps))
    return lax.ppermute(value, axis, [(source, source + steps) for source in range(leading, last)])


def gelu_exact(values):
    return 0.5 * values * (1.0 + lax.erf(values * SQRT_HALF))


def gelu_slope(values):
    cumulative = 0.5 * (1.0 + lax.erf(values * SQRT_HALF))
    density = jnp.exp(-0.5 * values * values) * INV_ROOT_TAU
    return cumulative + values * density


def wide_patches(signal, first_next):
    recs_local, length, channels = signal.shape
    paired = signal.reshape(recs_local, length // 2, 2 * channels)
    following = jnp.concatenate([paired[:, 1:, :channels], first_next], axis=1)
    return jnp.concatenate([paired, following], axis=2)


def narrow_patches(signal):
    recs_local, length, channels = signal.shape
    return signal.reshape(recs_local, length // 2, 2 * channels)


def conv_forward(patches, weight, bias_conv, gain_row, bias_row):
    recs_local, out_rows, patch_width = patches.shape
    conv_out = jnp.dot(
        patches.reshape(recs_local * out_rows, patch_width),
        weight,
        preferred_element_type=jnp.float32,
    )
    conv_out = conv_out.reshape(recs_local, out_rows, weight.shape[1]) + bias_conv
    center = jnp.mean(conv_out, axis=2, keepdims=True)
    centered = conv_out - center
    inverse = lax.rsqrt(jnp.mean(centered * centered, axis=2, keepdims=True) + EPSILON)
    normed = centered * inverse
    preact = normed * gain_row + bias_row
    activated = gelu_exact(preact).astype(jnp.bfloat16)
    return (activated, (patches, normed, preact, inverse))


def conv_backward(grad_act, weight, gain_row, stored):
    patches, normed, preact, inverse = stored
    recs_local, out_rows, patch_width = patches.shape
    grad_normed = grad_act.astype(jnp.float32) * gelu_slope(preact) * gain_row
    avg_grad = jnp.mean(grad_normed, axis=2, keepdims=True)
    avg_cross = jnp.mean(grad_normed * normed, axis=2, keepdims=True)
    grad_conv = (inverse * (grad_normed - avg_grad - normed * avg_cross)).astype(jnp.bfloat16)
    flat_patches = patches.reshape(recs_local * out_rows, patch_width)
    flat_grad = grad_conv.reshape(recs_local * out_rows, weight.shape[1])
    weight_grad = lax.dot_general(
        flat_patches, flat_grad, (((0,), (0,)), ((), ())), preferred_element_type=jnp.float32
    )
    grad_patch = lax.dot_general(
        flat_grad, weight, (((1,), (1,)), ((), ())), preferred_element_type=jnp.float32
    )
    return (weight_grad, grad_patch.reshape(recs_local, out_rows, patch_width))


def wide_input_grad(grad_patch, channels):
    recs_local, out_rows, patch_width = grad_patch.shape
    tail = grad_patch[:, :, 2 * channels :]
    incoming = passed_along(tail[:, -1:], "tm", 1)
    shifted = jnp.concatenate([incoming, tail[:, :-1]], axis=1)
    first_half = grad_patch[:, :, :channels] + shifted
    combined = jnp.concatenate([first_half, grad_patch[:, :, channels : 2 * channels]], axis=2)
    return combined.reshape(recs_local, 2 * out_rows, channels).astype(jnp.bfloat16)


def narrow_input_grad(grad_patch, channels):
    recs_local, out_rows, patch_width = grad_patch.shape
    return grad_patch.reshape(recs_local, 2 * out_rows, channels).astype(jnp.bfloat16)


def share_grad(weight_grad, factor):
    flat = (weight_grad * factor).reshape(-1)
    result = lax.psum_scatter(flat, ("dp", "tm"), scatter_dimension=0, tiled=True)
    return result


def generic_shards(
    features,
    conv_wide,
    conv_narrow,
    conv_bias,
    norm_gain,
    norm_bias,
    proj_gain,
    proj_weight,
    proj_bias,
    upstream,
):
    recs_local, length, channels = features.shape
    tm_count = lax.axis_size("tm")
    frames_total = upstream.shape[1]
    frames_local = frames_total // tm_count
    factor = 1.0 / math.sqrt(recs_local * lax.axis_size("dp") * frames_total)
    grad_frames = lax.all_to_all(upstream, "tm", split_axis=1, concat_axis=0, tiled=True)
    first_next = passed_along(features[:, :1], "tm", -1)
    act_wide, stored_wide = conv_forward(
        wide_patches(features, first_next), conv_wide, conv_bias[0], norm_gain[0], norm_bias[0]
    )
    act_narrow, stored_narrow = conv_forward(
        narrow_patches(act_wide), conv_narrow, conv_bias[1], norm_gain[1], norm_bias[1]
    )
    widened = act_narrow.astype(jnp.float32)
    centered = widened - jnp.mean(widened, axis=2, keepdims=True)
    row_inverse = lax.rsqrt(jnp.mean(centered * centered, axis=2, keepdims=True) + EPSILON)
    unit_rows = centered * row_inverse
    normed_in = (unit_rows * proj_gain).astype(jnp.bfloat16)
    weight_heads = proj_weight.reshape(channels, HEADS, HEAD_DIM)
    projected = jnp.einsum(
        "rfc,chd->rhfd", normed_in, weight_heads, preferred_element_type=jnp.float32
    ) + proj_bias.reshape(HEADS, 1, HEAD_DIM)
    heads_local = projected.astype(jnp.bfloat16).reshape(recs_local * HEADS, frames_local, HEAD_DIM)
    attn_input = lax.all_to_all(heads_local, "tm", split_axis=0, concat_axis=1, tiled=True)
    grad_heads = grad_frames.reshape(recs_local, HEADS, frames_local, HEAD_DIM)
    grad_unit = (
        jnp.einsum("rhfd,chd->rfc", grad_heads, weight_heads, preferred_element_type=jnp.float32)
        * proj_gain
    )
    grad_last = (
        row_inverse
        * (
            grad_unit
            - jnp.mean(grad_unit, axis=2, keepdims=True)
            - unit_rows * jnp.mean(grad_unit * unit_rows, axis=2, keepdims=True)
        )
    ).astype(jnp.bfloat16)
    weight_narrow, patch_narrow = conv_backward(grad_last, conv_narrow, norm_gain[1], stored_narrow)
    grad_conv_narrow = share_grad(weight_narrow, factor)
    grad_first = narrow_input_grad(patch_narrow, channels)
    weight_wide, patch_wide = conv_backward(grad_first, conv_wide, norm_gain[0], stored_wide)
    grad_conv_wide = share_grad(weight_wide, factor)
    feature_grad = wide_input_grad(patch_wide, channels)
    return (attn_input, feature_grad, grad_conv_wide, grad_conv_narrow)


F32 = jnp.float32
ORDER = (0, 7, 6, 4, 5, 3, 2, 1)
BF16 = jnp.bfloat16
NT = (((1,), (1,)), ((), ()))


def dot(a, b):
    return jnp.dot(a, b, preferred_element_type=F32)


def dot_nt(a, b):
    return lax.dot_general(a, b, NT, preferred_element_type=F32)


def row_mean(values):
    return jnp.mean(values, axis=1, keepdims=True)


def normalized(values):
    centered = values - row_mean(values)
    inverse = lax.rsqrt(row_mean(centered * centered) + EPSILON)
    return centered * inverse, inverse


def gelu_parts(preact):
    cumulative = 0.5 * (1.0 + lax.erf(preact * SQRT_HALF))
    slope = cumulative + preact * (jnp.exp(-0.5 * preact * preact) * INV_ROOT_TAU)
    return preact * cumulative, slope


def local(kernel, operands, outs, name, limit=16, scratch=(), raw=(), raw_out=(), free=(), aliases=None, cost=1000):
    out_shape, out_specs = [], []
    for number, (shape, dtype, stays) in enumerate(outs):
        out_shape.append((pltpu.VMEM if stays else pltpu.HBM)(shape, dtype))
        out_specs.append(pl.BlockSpec(memory_space=pltpu.HBM if number in raw_out else pltpu.VMEM))
    held = [
        x if k in free else pltpu.with_memory_space_constraint(x, pltpu.HBM if k in raw else pltpu.VMEM)
        for k, x in enumerate(operands)
    ]
    return pl.pallas_call(
        kernel,
        out_shape=out_shape,
        in_specs=[
            pl.BlockSpec(memory_space=pl.ANY if k in free else pltpu.HBM if k in raw else pltpu.VMEM)
            for k in range(len(operands))
        ],
        out_specs=out_specs,
        scratch_shapes=list(scratch),
        input_output_aliases=aliases or {},
        compiler_params=pltpu.CompilerParams(vmem_limit_bytes=limit << 20),
        cost_estimate=pl.CostEstimate(flops=cost, bytes_accessed=0, transcendentals=0),
        name=name,
    )(*held)


def run_copies(pairs, sems):
    copies = [pltpu.make_async_copy(src, dst, sems.at[k]) for k, (src, dst) in enumerate(pairs)]
    for copy in copies:
        copy.start()
    for copy in copies:
        copy.wait()


def first_cut_kernel(flips, whole, signal, *refs):
    *parts, first_rows, sems = refs
    width = parts[0].shape[2]
    own = lax.axis_index("tm")
    starts = [pl.multiple_of((own ^ flip) * width, width) for flip in flips]
    pairs = [(whole.at[:, :, pl.ds(start, width)], part) for start, part in zip(starts, parts)]
    run_copies([*pairs, (signal.at[pl.ds(0, 8), :], first_rows)], sems)


def rest_cut_kernel(flips, whole, *refs):
    *parts, held, sems, out_sems = refs
    width = held.shape[3]
    own = lax.axis_index("tm")
    reads, writes = [], []
    for k, flip in enumerate(flips):
        start = pl.multiple_of((own ^ flip) * width, width)
        reads.append(pltpu.make_async_copy(whole.at[:, :, pl.ds(start, width)], held.at[k], sems.at[k]))
        writes.append(pltpu.make_async_copy(held.at[k], parts[k], out_sems.at[k]))
    for read in reads:
        read.start()
    for read, write in zip(reads, writes):
        read.wait()
        write.start()
    for write in writes:
        write.wait()


def join_kernel(parts, whole, sems):
    width = parts.shape[3]
    run_copies([(parts.at[k], whole.at[:, :, pl.ds(k * width, width)]) for k in range(parts.shape[0])], sems)


class Loads:
    def __init__(self, sources, held, sems):
        self.pairs = [
            (pltpu.make_async_copy(src, buf, sems.at[k]), buf) for k, (src, buf) in enumerate(zip(sources, held))
        ]
        for read, _ in self.pairs:
            read.start()

    def take(self, count):
        taken, self.pairs = self.pairs[:count], self.pairs[count:]
        for read, _ in taken:
            read.wait()
        return [buf for _, buf in taken]


def spread_rows(spread, first, count):
    lanes = [spread[lane, pl.ds(first, count, stride=4), :] for lane in range(spread.shape[0])]
    return jnp.concatenate(lanes, axis=1)


def put_rows(spread, first, value):
    for lane in range(spread.shape[0]):
        spread[lane, pl.ds(first, value.shape[0], stride=4), :] = value[:, lane * 128 : (lane + 1) * 128]


def forward_kernel(*refs):
    sources, outs, rest = refs[:10], refs[10:21], refs[21:]
    *held, sems, out_sems, spread, patches = rest
    held, bufs = held[:10], held[10:]
    writes = []

    def put(number):
        write = pltpu.make_async_copy(bufs[number], outs[number], out_sems.at[number])
        write.start()
        writes.append(write)

    (
        proj_t,
        patch_t,
        act_t,
        normed_w,
        slope_w,
        inv_w,
        normed_n,
        slope_n,
        inv_n,
        unit_out,
        row_inv,
    ) = bufs
    loads = Loads(sources, held, sems)
    feat, halo, conv_bias, norm_gain, norm_bias = loads.take(5)
    frames = feat.shape[0] // 4
    channels = feat.shape[1]
    for lane in range(channels // 128):
        spread[lane] = feat[:, lane * 128 : (lane + 1) * 128].astype(F32)
    rows = [spread_rows(spread, j, frames) for j in range(4)]
    following = pltpu.roll(rows[0], frames - 1, axis=0)
    at_end = lax.broadcasted_iota(jnp.int32, (frames, 1), 0) == frames - 1
    rows.append(jnp.where(at_end, halo[0:1, :].astype(F32), following))
    rows = [row.astype(BF16) for row in rows]
    for parity in range(2):
        for tap in range(3):
            piece = rows[2 * parity + tap]
            patches[parity * frames : (parity + 1) * frames, tap * channels : (tap + 1) * channels] = piece
            patch_t[tap * channels : (tap + 1) * channels, parity * frames : (parity + 1) * frames] = piece.T
    put(1)
    (conv_wide,) = loads.take(1)
    conv = dot(patches[...], conv_wide[...]) + conv_bias[0:1, :]
    normed, inverse = normalized(conv)
    normed_w[...] = normed
    inv_w[...] = jnp.broadcast_to(inverse, inv_w.shape)
    put(3)
    put(5)
    act, slope = gelu_parts(normed * norm_gain[0:1, :] + norm_bias[0:1, :])
    slope_w[...] = slope * norm_gain[0:1, :]
    put(4)
    act = act.astype(BF16)
    even, odd = act[:frames], act[frames:]
    act_t[0:channels, :] = even.T
    act_t[channels:, :] = odd.T
    put(2)
    (conv_narrow,) = loads.take(1)
    conv = dot(even, conv_narrow[0:channels, :]) + dot(odd, conv_narrow[channels:, :]) + conv_bias[1:2, :]
    normed, inverse = normalized(conv)
    normed_n[...] = normed
    inv_n[...] = jnp.broadcast_to(inverse, inv_n.shape)
    put(6)
    put(8)
    act, slope = gelu_parts(normed * norm_gain[1:2, :] + norm_bias[1:2, :])
    slope_n[...] = slope * norm_gain[1:2, :]
    put(7)
    unit, inverse = normalized(act.astype(BF16).astype(F32))
    unit_out[...] = unit
    row_inv[...] = jnp.broadcast_to(inverse, row_inv.shape)
    put(9)
    put(10)
    proj_gain, proj_bias, proj_weight = loads.take(3)
    normed_in = (unit * proj_gain[...]).astype(BF16)
    bias = jnp.concatenate([proj_bias[k : k + 1, :] for k in range(proj_bias.shape[0])], axis=1)
    projected = dot(normed_in, proj_weight[...]) + bias
    proj_t[...] = projected.astype(BF16).T
    put(0)
    for write in writes:
        write.wait()


def owned_rows(left, owner, outer):
    part = left.shape[0] // (2 * outer)
    return [left.at[pl.ds(pl.multiple_of((2 * block + owner) * part, part), part), :] for block in range(outer)]


def weight_grad(loads, grad, factor, target, low):
    outer, inner, height = target.shape[0], target.shape[1], target.shape[2]
    for block, left in enumerate(loads.take(outer)):
        value = (dot(left[...], grad) * factor).astype(BF16)
        each = left.shape[0] // inner
        row = height - each if low else 0
        for k in range(inner):
            target[block, k, row : row + each, :] = value[k * each : (k + 1) * each]


def backward_kernel(factor, *refs):
    tm = lax.axis_size("tm")
    count = 13 + tm
    sources, (send, grad_conv, grad_low), rest = refs[:count], refs[count : count + 3], refs[count + 3 :]
    *held, grad_t, sems = rest
    outer = send.shape[0]
    own = lax.axis_index("tm")
    rows = sources[1].shape[0]
    places = [grad_t.at[pl.ds(pl.multiple_of((own ^ k) * rows, rows), rows), :] for k in ORDER]
    other = 1 - lax.axis_index("dp") % 2
    wide_left, low_left = (owned_rows(left, other, outer) for left in sources[-2:])
    cut = held[0].shape[1] * 8 // 15
    halves = [pl.ds(0, cut), pl.ds(cut, held[0].shape[1] - cut)]
    loads = Loads([*sources[1 : 1 + tm], *(sources[0].at[:, at] for at in halves), *sources[1 + tm : -5], *low_left, *sources[-5:-2], *wide_left], [*places, *(held[0].at[:, at] for at in halves), *held[1:]], sems)
    loads.take(tm)
    product = dot(loads.take(1)[0][...], grad_t[0:cut, :])
    right, proj_gain = loads.take(2)
    grad_unit = (product + dot(right[...], grad_t[cut:, :])).T * proj_gain[...]
    unit_in, row_inv = loads.take(2)
    frames, channels = unit_in.shape
    unit = unit_in[...]
    grad_last = row_inv[:, 0:1] * (grad_unit - row_mean(grad_unit) - unit * row_mean(grad_unit * unit))
    normed_n, slope_n, inv_n, conv_narrow = loads.take(4)
    grad_normed = grad_last.astype(BF16).astype(F32) * slope_n[...]
    normed = normed_n[...]
    grad_narrow = (
        inv_n[:, 0:1] * (grad_normed - row_mean(grad_normed) - normed * row_mean(grad_normed * normed))
    ).astype(BF16)
    grad_low[...] = grad_narrow
    weight_grad(loads, grad_narrow, factor, send, True)
    normed_w, slope_w, inv_w = loads.take(3)
    for parity in range(2):
        at = pl.ds(parity * frames, frames)
        grad_first = dot_nt(grad_narrow, conv_narrow[parity * channels : (parity + 1) * channels, :]).astype(BF16)
        grad_normed = grad_first.astype(F32) * slope_w[at, :]
        normed = normed_w[at, :]
        grad_conv[at, :] = (
            inv_w[at, 0:1] * (grad_normed - row_mean(grad_normed) - normed * row_mean(grad_normed * normed))
        ).astype(BF16)
    weight_grad(loads, grad_conv[...], factor, send, False)


def own_grad_kernel(factor, patch_t, act_t, conv_wide, grad_conv, grad_low, keep, tail, *rest):
    held, sems = rest[:-1], rest[-1]
    outer = keep.shape[0]
    core = lax.axis_index("dp") % 2
    lefts = [rows for left in (patch_t, act_t) for rows in owned_rows(left, core, outer)]
    last_tap = held[-1].shape[0]
    loads = Loads([*lefts, conv_wide.at[pl.ds(2 * last_tap, last_tap), :]], held, sems)
    grad_wide = grad_conv[...]
    weight_grad(loads, grad_wide, factor, keep, False)
    weight_grad(loads, grad_low[...], factor, keep, True)
    (tap,) = loads.take(1)
    tail[...] = dot_nt(grad_wide[grad_wide.shape[0] - 8 :, :], tap[...])


def input_grad_kernel(grad_conv, conv_wide, out, first_rows, spread):
    frames = grad_conv.shape[0] // 2
    channels = grad_conv.shape[1]
    even, odd = grad_conv[:frames, :], grad_conv[frames:, :]
    taps = [conv_wide[tap * channels : (tap + 1) * channels, :] for tap in range(3)]
    shifted = pltpu.roll(dot_nt(odd, taps[2]), 1, axis=0)
    at_start = lax.broadcasted_iota(jnp.int32, (frames, 1), 0) == 0
    shifted = jnp.where(at_start, 0.0, shifted)
    put_rows(spread, 0, dot_nt(even, taps[0]) + shifted)
    put_rows(spread, 1, dot_nt(even, taps[1]))
    put_rows(spread, 2, dot_nt(even, taps[2]) + dot_nt(odd, taps[0]))
    put_rows(spread, 3, dot_nt(odd, taps[1]))
    for lane in range(channels // 128):
        out[:, lane * 128 : (lane + 1) * 128] = spread[lane].astype(BF16)
        first_rows[:, lane * 128 : (lane + 1) * 128] = spread[lane, 0:8, :]


def first_sum_kernel(keep, received, *outs):
    y = lax.axis_index("dp") // 2
    x = lax.axis_index("tm") % 2
    inner = keep.shape[1] // 2
    for flip, out in enumerate(outs):
        block = y ^ (flip // 2)
        lane = x ^ (flip % 2)
        for z in range(inner):
            at = 2 * z + lane
            out[z] = (keep[block, at].astype(F32) + received[block, at].astype(F32)).astype(BF16)


def second_sum_kernel(a, b, c, d, *outs):
    z = lax.axis_index("tm") // 2
    for flip, out in enumerate(outs):
        at = z ^ flip
        total = (a[at].astype(F32) + b[at].astype(F32)) + (c[at].astype(F32) + d[at].astype(F32))
        out[...] = total.astype(BF16)


def last_sum_kernel(wide_rows, a, b, c, d, incoming, first_rows, grad_in, wide, narrow, grad_out, rows_buf, sem):
    at_start = lax.broadcasted_iota(jnp.int32, (8, 1), 0) == 0
    rows_buf[...] = (first_rows[...] + jnp.where(at_start, incoming[7:8, :], 0.0)).astype(BF16)
    put = pltpu.make_async_copy(rows_buf, grad_out.at[pl.ds(0, 8), :], sem)
    put.start()
    total = (a[...].astype(F32) + b[...].astype(F32)) + (c[...].astype(F32) + d[...].astype(F32))
    rows, channels = total.shape
    pieces = channels // 128
    for p in range(pieces):
        lanes = total[:, p * 128 : (p + 1) * 128]
        wide[pl.ds(p, wide_rows, stride=pieces), :] = lanes[:wide_rows]
        narrow[pl.ds(p, rows - wide_rows, stride=pieces), :] = lanes[wide_rows:]
    put.wait()


def flipped(dy, dc, dz, dx):
    dp, tm = lax.axis_size("dp"), lax.axis_size("tm")
    change_dp, change_tm = 2 * dy + dc, 2 * dz + dx
    return [
        (p * tm + t, (p ^ change_dp) * tm + (t ^ change_tm)) for p in range(dp) for t in range(tm)
    ]


def swap(value, dy, dc, dz, dx):
    return lax.ppermute(value, ("dp", "tm"), flipped(dy, dc, dz, dx))


def shards(
    features,
    conv_wide,
    conv_narrow,
    conv_bias,
    norm_gain,
    norm_bias,
    proj_gain,
    proj_weight,
    proj_bias,
    upstream,
):
    dp, tm = lax.axis_size("dp"), lax.axis_size("tm")
    recs_local, length, channels = features.shape
    pairs, frames_total, depth = upstream.shape
    frames = frames_total // tm
    if not (dp == 4 and tm == 8 and recs_local == 1 and frames % 128 == 0 and HEADS * depth % 128 == 0 and pairs * tm == HEADS):
        return generic_shards(
            features,
            conv_wide,
            conv_narrow,
            conv_bias,
            norm_gain,
            norm_bias,
            proj_gain,
            proj_weight,
            proj_bias,
            upstream,
        )
    width = HEADS * depth
    factor = 1.0 / math.sqrt(recs_local * dp * frames_total)
    sems = [pltpu.SemaphoreType.DMA((tm,))]
    signal = features.reshape(length, channels)
    frames_cut = (pairs, depth, frames)
    early = (1, 7)
    late = [k for k in range(tm) if k not in early]
    *cuts, first_rows = local(
        lambda *refs: first_cut_kernel(early, *refs),
        [upstream.transpose(0, 2, 1), signal],
        [(frames_cut, BF16, True)] * len(early) + [((8, channels), BF16, True)],
        "cut",
        scratch=[pltpu.SemaphoreType.DMA((len(early) + 1,))],
        raw=(0, 1),
    )
    cuts += local(
        lambda *refs: rest_cut_kernel(late, *refs),
        [upstream.transpose(0, 2, 1)],
        [(frames_cut, BF16, False)] * len(late),
        "rest_cut",
        scratch=[pltpu.VMEM((len(late), *frames_cut), BF16)] + [pltpu.SemaphoreType.DMA((len(late),))] * 2,
        raw=(0,),
        raw_out=range(len(late)),
    )
    cuts = {k: cut.reshape(pairs * depth, frames) for k, cut in zip([*early, *late], cuts)}
    heads_in = {0: cuts[0]}
    for k in ORDER[1:]:
        heads_in[k] = swap(cuts[k], 0, 0, k // 2, k % 2)
    halo = passed_along(first_rows, "tm", -1)
    wide_rows = 2 * frames
    spread = pltpu.VMEM((channels // 128, length, 128), F32)
    gain = proj_gain.reshape(1, channels)
    forward_in = [
        signal,
        halo,
        conv_bias,
        norm_gain,
        norm_bias,
        conv_wide,
        conv_narrow,
        gain,
        proj_bias.reshape(width // 128, 128),
        proj_weight,
    ]
    forward_out = [
        ((width, frames), BF16, False),
        ((3 * channels, wide_rows), BF16, False),
        ((2 * channels, frames), BF16, False),
        ((wide_rows, channels), F32, False),
        ((wide_rows, channels), F32, False),
        ((wide_rows, 128), F32, False),
        ((frames, channels), F32, False),
        ((frames, channels), F32, False),
        ((frames, 128), F32, False),
        ((frames, channels), F32, False),
        ((frames, 128), F32, False),
    ]
    proj_t, *stored = local(
        forward_kernel,
        forward_in,
        forward_out,
        "forward",
        limit=40,
        scratch=[pltpu.VMEM(x.shape, x.dtype) for x in forward_in]
        + [pltpu.VMEM(shape, dtype) for shape, dtype, _ in forward_out]
        + [
            pltpu.SemaphoreType.DMA((len(forward_in),)),
            pltpu.SemaphoreType.DMA((len(forward_out),)),
            spread,
            pltpu.VMEM((wide_rows, 3 * channels), BF16),
        ],
        raw=range(len(forward_in)),
        raw_out=range(len(forward_out)),
    )
    proj_t, heads_in[1] = lax.optimization_barrier((proj_t, heads_in[1]))
    heads = lax.all_to_all(
        proj_t.reshape(tm, pairs * depth, frames), "tm", split_axis=0, concat_axis=0, tiled=True
    )
    outer, inner = dp // 2, tm
    part_rows = 5 * channels // (dp * tm)
    part = ((outer, inner, part_rows, channels), BF16, True)
    patch_t, act_t, normed_w, slope_w, inv_w, normed_n, slope_n, inv_n, unit, row_inv = stored
    inputs = [
        proj_weight,
        *[heads_in[k] for k in ORDER],
        gain,
        unit,
        row_inv,
        normed_n,
        slope_n,
        inv_n,
        conv_narrow,
        normed_w,
        slope_w,
        inv_w,
        patch_t,
        act_t,
    ]
    lefts = [
        pltpu.VMEM((x.shape[0] // (2 * outer), x.shape[1]), BF16)
        for x in (patch_t, act_t)
        for _ in range(outer)
    ]
    held = [pltpu.VMEM(x.shape, x.dtype) for x in inputs[:1] + inputs[tm + 1 : -2]]
    held = held[:-3] + lefts[outer:] + held[-3:] + lefts[:outer]
    grad_buf = pltpu.VMEM((width, frames), BF16)
    send, grad_conv, grad_low = local(
        lambda *refs: backward_kernel(factor, *refs),
        inputs,
        [part, ((wide_rows, channels), BF16, True), ((frames, channels), BF16, True)],
        "backward",
        limit=24,
        scratch=held + [grad_buf, pltpu.SemaphoreType.DMA((len(held) + tm + 1,))],
        raw=range(len(inputs)),
        free=range(1, tm + 1),
    )
    received = swap(send, 0, 1, 0, 0)
    held = lefts + [pltpu.VMEM((channels, channels), BF16)]
    keep, tail = local(
        lambda *refs: own_grad_kernel(factor, *refs),
        [patch_t, act_t, conv_wide, grad_conv, grad_low],
        [part, ((8, channels), F32, True)],
        "own_grad",
        scratch=held + [pltpu.SemaphoreType.DMA((len(held),))],
        raw=(0, 1, 2),
    )
    plane = ((tm // 2, part_rows, channels), BF16, True)
    own, *outgoing = local(first_sum_kernel, [keep, received], [plane] * 4, "first_sum")
    arrived = [swap(outgoing[k - 1], k // 2, 0, 0, k % 2) for k in (3,2,1)]
    tail, grad_conv, own = lax.optimization_barrier((tail, grad_conv, own))
    incoming = passed_along(tail, "tm", 1)
    feature_grad, first_rows = local(
        input_grad_kernel,
        [grad_conv, conv_wide],
        [((length, channels), BF16, False), ((8, channels), F32, True)],
        "input_grad",
        scratch=[spread],
    )
    piece = ((part_rows, channels), BF16, True)
    (attn_t,) = local(
        join_kernel,
        [heads.reshape(tm, pairs, depth, frames)],
        [((pairs, depth, frames_total), BF16, False)],
        "join",
        scratch=sems,
        raw_out=(0,),
    )
    attn_t, first_rows, incoming, own = lax.optimization_barrier((attn_t, first_rows, incoming, own))
    own, *outgoing = local(second_sum_kernel, [own, *arrived], [piece] * 4, "second_sum")
    arrived = [swap(outgoing[k - 1], 0, 0, k, 0) for k in (2,1,3)]
    own_wide = 3 * channels // (dp * tm)
    wide, narrow, feature_grad = local(
        lambda *refs: last_sum_kernel(own_wide, *refs),
        [own, *arrived, incoming, first_rows, feature_grad],
        [
            ((own_wide * channels // 128, 128), F32, False),
            (((part_rows - own_wide) * channels // 128, 128), F32, False),
            ((length, channels), BF16, False),
        ],
        "last_sum",
        scratch=[pltpu.VMEM((8, channels), BF16), pltpu.SemaphoreType.DMA(())],
        raw=(6,),
        raw_out=(2,),
        aliases={6: 2},
    )
    return (
        attn_t.transpose(0, 2, 1),
        feature_grad.reshape(recs_local, length, channels),
        wide.reshape(-1),
        narrow.reshape(-1),
    )


def solution(mesh):
    in_specs = (
        P("dp", "tm", None),
        P(),
        P(),
        P(),
        P(),
        P(),
        P(),
        P(),
        P(),
        P(("dp", "tm"), None, None),
    )
    out_specs = (P(("dp", "tm"), None, None), P("dp", "tm", None), P(("dp", "tm")), P(("dp", "tm")))
    return jax.shard_map(shards, mesh=mesh, in_specs=in_specs, out_specs=out_specs, check_vma=False)
```

```python
import math

import jax
import jax.numpy as jnp
from jax import lax
from jax.experimental import pallas as pl
from jax.experimental.pallas import tpu as pltpu
from jax.sharding import PartitionSpec as P

HEADS = 16
HEAD_DIM = 120


EPSILON = 1e-05
SQRT_HALF = 0.7071067811865476
INV_ROOT_TAU = 0.3989422804014327


def passed_along(value, axis, steps):
    count = lax.axis_size(axis)
    leading, last = (max(0, -steps), min(count, count - steps))
    return lax.ppermute(value, axis, [(source, source + steps) for source in range(leading, last)])


def gelu_exact(values):
    return 0.5 * values * (1.0 + lax.erf(values * SQRT_HALF))


def gelu_slope(values):
    cumulative = 0.5 * (1.0 + lax.erf(values * SQRT_HALF))
    density = jnp.exp(-0.5 * values * values) * INV_ROOT_TAU
    return cumulative + values * density


def wide_patches(signal, first_next):
    recs_local, length, channels = signal.shape
    paired = signal.reshape(recs_local, length // 2, 2 * channels)
    following = jnp.concatenate([paired[:, 1:, :channels], first_next], axis=1)
    return jnp.concatenate([paired, following], axis=2)


def narrow_patches(signal):
    recs_local, length, channels = signal.shape
    return signal.reshape(recs_local, length // 2, 2 * channels)


def conv_forward(patches, weight, bias_conv, gain_row, bias_row):
    recs_local, out_rows, patch_width = patches.shape
    conv_out = jnp.dot(
        patches.reshape(recs_local * out_rows, patch_width),
        weight,
        preferred_element_type=jnp.float32,
    )
    conv_out = conv_out.reshape(recs_local, out_rows, weight.shape[1]) + bias_conv
    center = jnp.mean(conv_out, axis=2, keepdims=True)
    centered = conv_out - center
    inverse = lax.rsqrt(jnp.mean(centered * centered, axis=2, keepdims=True) + EPSILON)
    normed = centered * inverse
    preact = normed * gain_row + bias_row
    activated = gelu_exact(preact).astype(jnp.bfloat16)
    return (activated, (patches, normed, preact, inverse))


def conv_backward(grad_act, weight, gain_row, stored):
    patches, normed, preact, inverse = stored
    recs_local, out_rows, patch_width = patches.shape
    grad_normed = grad_act.astype(jnp.float32) * gelu_slope(preact) * gain_row
    avg_grad = jnp.mean(grad_normed, axis=2, keepdims=True)
    avg_cross = jnp.mean(grad_normed * normed, axis=2, keepdims=True)
    grad_conv = (inverse * (grad_normed - avg_grad - normed * avg_cross)).astype(jnp.bfloat16)
    flat_patches = patches.reshape(recs_local * out_rows, patch_width)
    flat_grad = grad_conv.reshape(recs_local * out_rows, weight.shape[1])
    weight_grad = lax.dot_general(
        flat_patches, flat_grad, (((0,), (0,)), ((), ())), preferred_element_type=jnp.float32
    )
    grad_patch = lax.dot_general(
        flat_grad, weight, (((1,), (1,)), ((), ())), preferred_element_type=jnp.float32
    )
    return (weight_grad, grad_patch.reshape(recs_local, out_rows, patch_width))


def wide_input_grad(grad_patch, channels):
    recs_local, out_rows, patch_width = grad_patch.shape
    tail = grad_patch[:, :, 2 * channels :]
    incoming = passed_along(tail[:, -1:], "tm", 1)
    shifted = jnp.concatenate([incoming, tail[:, :-1]], axis=1)
    first_half = grad_patch[:, :, :channels] + shifted
    combined = jnp.concatenate([first_half, grad_patch[:, :, channels : 2 * channels]], axis=2)
    return combined.reshape(recs_local, 2 * out_rows, channels).astype(jnp.bfloat16)


def narrow_input_grad(grad_patch, channels):
    recs_local, out_rows, patch_width = grad_patch.shape
    return grad_patch.reshape(recs_local, 2 * out_rows, channels).astype(jnp.bfloat16)


def share_grad(weight_grad, factor):
    flat = (weight_grad * factor).reshape(-1)
    result = lax.psum_scatter(flat, ("dp", "tm"), scatter_dimension=0, tiled=True)
    return result


def generic_shards(
    features,
    conv_wide,
    conv_narrow,
    conv_bias,
    norm_gain,
    norm_bias,
    proj_gain,
    proj_weight,
    proj_bias,
    upstream,
):
    recs_local, length, channels = features.shape
    tm_count = lax.axis_size("tm")
    frames_total = upstream.shape[1]
    frames_local = frames_total // tm_count
    factor = 1.0 / math.sqrt(recs_local * lax.axis_size("dp") * frames_total)
    grad_frames = lax.all_to_all(upstream, "tm", split_axis=1, concat_axis=0, tiled=True)
    first_next = passed_along(features[:, :1], "tm", -1)
    act_wide, stored_wide = conv_forward(
        wide_patches(features, first_next), conv_wide, conv_bias[0], norm_gain[0], norm_bias[0]
    )
    act_narrow, stored_narrow = conv_forward(
        narrow_patches(act_wide), conv_narrow, conv_bias[1], norm_gain[1], norm_bias[1]
    )
    widened = act_narrow.astype(jnp.float32)
    centered = widened - jnp.mean(widened, axis=2, keepdims=True)
    row_inverse = lax.rsqrt(jnp.mean(centered * centered, axis=2, keepdims=True) + EPSILON)
    unit_rows = centered * row_inverse
    normed_in = (unit_rows * proj_gain).astype(jnp.bfloat16)
    weight_heads = proj_weight.reshape(channels, HEADS, HEAD_DIM)
    projected = jnp.einsum(
        "rfc,chd->rhfd", normed_in, weight_heads, preferred_element_type=jnp.float32
    ) + proj_bias.reshape(HEADS, 1, HEAD_DIM)
    heads_local = projected.astype(jnp.bfloat16).reshape(recs_local * HEADS, frames_local, HEAD_DIM)
    attn_input = lax.all_to_all(heads_local, "tm", split_axis=0, concat_axis=1, tiled=True)
    grad_heads = grad_frames.reshape(recs_local, HEADS, frames_local, HEAD_DIM)
    grad_unit = (
        jnp.einsum("rhfd,chd->rfc", grad_heads, weight_heads, preferred_element_type=jnp.float32)
        * proj_gain
    )
    grad_last = (
        row_inverse
        * (
            grad_unit
            - jnp.mean(grad_unit, axis=2, keepdims=True)
            - unit_rows * jnp.mean(grad_unit * unit_rows, axis=2, keepdims=True)
        )
    ).astype(jnp.bfloat16)
    weight_narrow, patch_narrow = conv_backward(grad_last, conv_narrow, norm_gain[1], stored_narrow)
    grad_conv_narrow = share_grad(weight_narrow, factor)
    grad_first = narrow_input_grad(patch_narrow, channels)
    weight_wide, patch_wide = conv_backward(grad_first, conv_wide, norm_gain[0], stored_wide)
    grad_conv_wide = share_grad(weight_wide, factor)
    feature_grad = wide_input_grad(patch_wide, channels)
    return (attn_input, feature_grad, grad_conv_wide, grad_conv_narrow)


F32 = jnp.float32
ORDER = (0, 7, 6, 4, 3, 5, 2, 1)
BF16 = jnp.bfloat16
NT = (((1,), (1,)), ((), ()))


def dot(a, b):
    return jnp.dot(a, b, preferred_element_type=F32)


def dot_nt(a, b):
    return lax.dot_general(a, b, NT, preferred_element_type=F32)


def row_mean(values):
    return jnp.mean(values, axis=1, keepdims=True)


def normalized(values):
    centered = values - row_mean(values)
    inverse = lax.rsqrt(row_mean(centered * centered) + EPSILON)
    return centered * inverse, inverse


def gelu_parts(preact):
    cumulative = 0.5 * (1.0 + lax.erf(preact * SQRT_HALF))
    slope = cumulative + preact * (jnp.exp(-0.5 * preact * preact) * INV_ROOT_TAU)
    return preact * cumulative, slope


def local(kernel, operands, outs, name, limit=16, scratch=(), raw=(), raw_out=(), free=(), aliases=None, cost=1000):
    out_shape, out_specs = [], []
    for number, (shape, dtype, stays) in enumerate(outs):
        out_shape.append((pltpu.VMEM if stays else pltpu.HBM)(shape, dtype))
        out_specs.append(pl.BlockSpec(memory_space=pltpu.HBM if number in raw_out else pltpu.VMEM))
    held = [
        x if k in free else pltpu.with_memory_space_constraint(x, pltpu.HBM if k in raw else pltpu.VMEM)
        for k, x in enumerate(operands)
    ]
    return pl.pallas_call(
        kernel,
        out_shape=out_shape,
        in_specs=[
            pl.BlockSpec(memory_space=pl.ANY if k in free else pltpu.HBM if k in raw else pltpu.VMEM)
            for k in range(len(operands))
        ],
        out_specs=out_specs,
        scratch_shapes=list(scratch),
        input_output_aliases=aliases or {},
        compiler_params=pltpu.CompilerParams(vmem_limit_bytes=limit << 20),
        cost_estimate=pl.CostEstimate(flops=cost, bytes_accessed=0, transcendentals=0),
        name=name,
    )(*held)


def run_copies(pairs, sems):
    copies = [pltpu.make_async_copy(src, dst, sems.at[k]) for k, (src, dst) in enumerate(pairs)]
    for copy in copies:
        copy.start()
    for copy in copies:
        copy.wait()


def first_cut_kernel(flips, whole, signal, *refs):
    *parts, first_rows, sems = refs
    width = parts[0].shape[2]
    own = lax.axis_index("tm")
    starts = [pl.multiple_of((own ^ flip) * width, width) for flip in flips]
    pairs = [(whole.at[:, :, pl.ds(start, width)], part) for start, part in zip(starts, parts)]
    run_copies([*pairs, (signal.at[pl.ds(0, 8), :], first_rows)], sems)


def rest_cut_kernel(flips, whole, *refs):
    *parts, held, sems, out_sems = refs
    width = held.shape[3]
    own = lax.axis_index("tm")
    reads, writes = [], []
    for k, flip in enumerate(flips):
        start = pl.multiple_of((own ^ flip) * width, width)
        reads.append(pltpu.make_async_copy(whole.at[:, :, pl.ds(start, width)], held.at[k], sems.at[k]))
        writes.append(pltpu.make_async_copy(held.at[k], parts[k], out_sems.at[k]))
    for read in reads:
        read.start()
    for read, write in zip(reads, writes):
        read.wait()
        write.start()
    for write in writes:
        write.wait()


def join_kernel(parts, whole, sems):
    width = parts.shape[3]
    run_copies([(parts.at[k], whole.at[:, :, pl.ds(k * width, width)]) for k in range(parts.shape[0])], sems)


class Loads:
    def __init__(self, sources, held, sems):
        self.pairs = [
            (pltpu.make_async_copy(src, buf, sems.at[k]), buf) for k, (src, buf) in enumerate(zip(sources, held))
        ]
        for read, _ in self.pairs:
            read.start()

    def take(self, count):
        taken, self.pairs = self.pairs[:count], self.pairs[count:]
        for read, _ in taken:
            read.wait()
        return [buf for _, buf in taken]


def spread_rows(spread, first, count):
    lanes = [spread[lane, pl.ds(first, count, stride=4), :] for lane in range(spread.shape[0])]
    return jnp.concatenate(lanes, axis=1)


def put_rows(spread, first, value):
    for lane in range(spread.shape[0]):
        spread[lane, pl.ds(first, value.shape[0], stride=4), :] = value[:, lane * 128 : (lane + 1) * 128]


def forward_kernel(*refs):
    sources, outs, rest = refs[:10], refs[10:21], refs[21:]
    *held, sems, out_sems, spread, patches = rest
    held, bufs = held[:10], held[10:]
    writes = []

    def put(number):
        write = pltpu.make_async_copy(bufs[number], outs[number], out_sems.at[number])
        write.start()
        writes.append(write)

    (
        proj_t,
        patch_t,
        act_t,
        normed_w,
        slope_w,
        inv_w,
        normed_n,
        slope_n,
        inv_n,
        unit_out,
        row_inv,
    ) = bufs
    loads = Loads(sources, held, sems)
    feat, halo, conv_bias, norm_gain, norm_bias = loads.take(5)
    frames = feat.shape[0] // 4
    channels = feat.shape[1]
    for lane in range(channels // 128):
        spread[lane] = feat[:, lane * 128 : (lane + 1) * 128].astype(F32)
    rows = [spread_rows(spread, j, frames) for j in range(4)]
    following = pltpu.roll(rows[0], frames - 1, axis=0)
    at_end = lax.broadcasted_iota(jnp.int32, (frames, 1), 0) == frames - 1
    rows.append(jnp.where(at_end, halo[0:1, :].astype(F32), following))
    rows = [row.astype(BF16) for row in rows]
    for parity in range(2):
        for tap in range(3):
            piece = rows[2 * parity + tap]
            patches[parity * frames : (parity + 1) * frames, tap * channels : (tap + 1) * channels] = piece
            patch_t[tap * channels : (tap + 1) * channels, parity * frames : (parity + 1) * frames] = piece.T
    put(1)
    (conv_wide,) = loads.take(1)
    conv = dot(patches[...], conv_wide[...]) + conv_bias[0:1, :]
    normed, inverse = normalized(conv)
    normed_w[...] = normed
    inv_w[...] = jnp.broadcast_to(inverse, inv_w.shape)
    put(3)
    put(5)
    act, slope = gelu_parts(normed * norm_gain[0:1, :] + norm_bias[0:1, :])
    slope_w[...] = slope * norm_gain[0:1, :]
    put(4)
    act = act.astype(BF16)
    even, odd = act[:frames], act[frames:]
    act_t[0:channels, :] = even.T
    act_t[channels:, :] = odd.T
    put(2)
    (conv_narrow,) = loads.take(1)
    conv = dot(even, conv_narrow[0:channels, :]) + dot(odd, conv_narrow[channels:, :]) + conv_bias[1:2, :]
    normed, inverse = normalized(conv)
    normed_n[...] = normed
    inv_n[...] = jnp.broadcast_to(inverse, inv_n.shape)
    put(6)
    put(8)
    act, slope = gelu_parts(normed * norm_gain[1:2, :] + norm_bias[1:2, :])
    slope_n[...] = slope * norm_gain[1:2, :]
    put(7)
    unit, inverse = normalized(act.astype(BF16).astype(F32))
    unit_out[...] = unit
    row_inv[...] = jnp.broadcast_to(inverse, row_inv.shape)
    put(9)
    put(10)
    proj_gain, proj_bias, proj_weight = loads.take(3)
    normed_in = (unit * proj_gain[...]).astype(BF16)
    bias = jnp.concatenate([proj_bias[k : k + 1, :] for k in range(proj_bias.shape[0])], axis=1)
    projected = dot(normed_in, proj_weight[...]) + bias
    proj_t[...] = projected.astype(BF16).T
    put(0)
    for write in writes:
        write.wait()


def owned_rows(left, owner, outer):
    part = left.shape[0] // (2 * outer)
    return [left.at[pl.ds(pl.multiple_of((2 * block + owner) * part, part), part), :] for block in range(outer)]


def weight_grad(loads, grad, factor, target, low):
    outer, inner, height = target.shape[0], target.shape[1], target.shape[2]
    for block, left in enumerate(loads.take(outer)):
        value = (dot(left[...], grad) * factor).astype(BF16)
        each = left.shape[0] // inner
        row = height - each if low else 0
        for k in range(inner):
            target[block, k, row : row + each, :] = value[k * each : (k + 1) * each]


def backward_kernel(factor, *refs):
    tm = lax.axis_size("tm")
    count = 13 + tm
    sources, (send, grad_conv, grad_low), rest = refs[:count], refs[count : count + 3], refs[count + 3 :]
    *held, grad_t, sems = rest
    outer = send.shape[0]
    own = lax.axis_index("tm")
    rows = sources[1].shape[0]
    places = [grad_t.at[pl.ds(pl.multiple_of((own ^ k) * rows, rows), rows), :] for k in ORDER]
    other = 1 - lax.axis_index("dp") % 2
    wide_left, low_left = (owned_rows(left, other, outer) for left in sources[-2:])
    cut = held[0].shape[1] * 8 // 15
    halves = [pl.ds(0, cut), pl.ds(cut, held[0].shape[1] - cut)]
    loads = Loads([*sources[1 : 1 + tm], *(sources[0].at[:, at] for at in halves), *sources[1 + tm : -5], *low_left, *sources[-5:-2], *wide_left], [*places, *(held[0].at[:, at] for at in halves), *held[1:]], sems)
    loads.take(tm)
    product = dot(loads.take(1)[0][...], grad_t[0:cut, :])
    right, proj_gain = loads.take(2)
    grad_unit = (product + dot(right[...], grad_t[cut:, :])).T * proj_gain[...]
    unit_in, row_inv = loads.take(2)
    frames, channels = unit_in.shape
    unit = unit_in[...]
    grad_last = row_inv[:, 0:1] * (grad_unit - row_mean(grad_unit) - unit * row_mean(grad_unit * unit))
    normed_n, slope_n, inv_n, conv_narrow = loads.take(4)
    grad_normed = grad_last.astype(BF16).astype(F32) * slope_n[...]
    normed = normed_n[...]
    grad_narrow = (
        inv_n[:, 0:1] * (grad_normed - row_mean(grad_normed) - normed * row_mean(grad_normed * normed))
    ).astype(BF16)
    grad_low[...] = grad_narrow
    weight_grad(loads, grad_narrow, factor, send, True)
    normed_w, slope_w, inv_w = loads.take(3)
    for parity in range(2):
        at = pl.ds(parity * frames, frames)
        grad_first = dot_nt(grad_narrow, conv_narrow[parity * channels : (parity + 1) * channels, :]).astype(BF16)
        grad_normed = grad_first.astype(F32) * slope_w[at, :]
        normed = normed_w[at, :]
        grad_conv[at, :] = (
            inv_w[at, 0:1] * (grad_normed - row_mean(grad_normed) - normed * row_mean(grad_normed * normed))
        ).astype(BF16)
    weight_grad(loads, grad_conv[...], factor, send, False)


def own_grad_kernel(factor, patch_t, act_t, conv_wide, grad_conv, grad_low, keep, tail, *rest):
    held, sems = rest[:-1], rest[-1]
    outer = keep.shape[0]
    core = lax.axis_index("dp") % 2
    lefts = [rows for left in (patch_t, act_t) for rows in owned_rows(left, core, outer)]
    last_tap = held[-1].shape[0]
    loads = Loads([*lefts, conv_wide.at[pl.ds(2 * last_tap, last_tap), :]], held, sems)
    grad_wide = grad_conv[...]
    weight_grad(loads, grad_wide, factor, keep, False)
    weight_grad(loads, grad_low[...], factor, keep, True)
    (tap,) = loads.take(1)
    tail[...] = dot_nt(grad_wide[grad_wide.shape[0] - 8 :, :], tap[...])


def input_grad_kernel(grad_conv, conv_wide, out, first_rows, spread):
    frames = grad_conv.shape[0] // 2
    channels = grad_conv.shape[1]
    even, odd = grad_conv[:frames, :], grad_conv[frames:, :]
    taps = [conv_wide[tap * channels : (tap + 1) * channels, :] for tap in range(3)]
    shifted = pltpu.roll(dot_nt(odd, taps[2]), 1, axis=0)
    at_start = lax.broadcasted_iota(jnp.int32, (frames, 1), 0) == 0
    shifted = jnp.where(at_start, 0.0, shifted)
    put_rows(spread, 0, dot_nt(even, taps[0]) + shifted)
    put_rows(spread, 1, dot_nt(even, taps[1]))
    put_rows(spread, 2, dot_nt(even, taps[2]) + dot_nt(odd, taps[0]))
    put_rows(spread, 3, dot_nt(odd, taps[1]))
    for lane in range(channels // 128):
        out[:, lane * 128 : (lane + 1) * 128] = spread[lane].astype(BF16)
        first_rows[:, lane * 128 : (lane + 1) * 128] = spread[lane, 0:8, :]


def first_sum_kernel(keep, received, *outs):
    y = lax.axis_index("dp") // 2
    x = lax.axis_index("tm") % 2
    inner = keep.shape[1] // 2
    for flip, out in enumerate(outs):
        block = y ^ (flip // 2)
        lane = x ^ (flip % 2)
        for z in range(inner):
            at = 2 * z + lane
            out[z] = (keep[block, at].astype(F32) + received[block, at].astype(F32)).astype(BF16)


def second_sum_kernel(a, b, c, d, *outs):
    z = lax.axis_index("tm") // 2
    for flip, out in enumerate(outs):
        at = z ^ flip
        total = (a[at].astype(F32) + b[at].astype(F32)) + (c[at].astype(F32) + d[at].astype(F32))
        out[...] = total.astype(BF16)


def first_row_kernel(incoming, first_rows, grad_in, grad_out, rows_buf, sem):
    at_start = lax.broadcasted_iota(jnp.int32, (8, 1), 0) == 0
    rows_buf[...] = (first_rows[...] + jnp.where(at_start, incoming[7:8, :], 0.0)).astype(BF16)
    run_copies([(rows_buf, grad_out.at[pl.ds(0, 8), :])], sem)


def last_sum_kernel(wide_rows, a, b, c, d, wide, narrow):
    total = (a[...].astype(F32) + b[...].astype(F32)) + (c[...].astype(F32) + d[...].astype(F32))
    rows, channels = total.shape
    pieces = channels // 128
    for p in range(pieces):
        lanes = total[:, p * 128 : (p + 1) * 128]
        wide[pl.ds(p, wide_rows, stride=pieces), :] = lanes[:wide_rows]
        narrow[pl.ds(p, rows - wide_rows, stride=pieces), :] = lanes[wide_rows:]


def flipped(dy, dc, dz, dx):
    dp, tm = lax.axis_size("dp"), lax.axis_size("tm")
    change_dp, change_tm = 2 * dy + dc, 2 * dz + dx
    return [
        (p * tm + t, (p ^ change_dp) * tm + (t ^ change_tm)) for p in range(dp) for t in range(tm)
    ]


def swap(value, dy, dc, dz, dx):
    return lax.ppermute(value, ("dp", "tm"), flipped(dy, dc, dz, dx))


def shards(
    features,
    conv_wide,
    conv_narrow,
    conv_bias,
    norm_gain,
    norm_bias,
    proj_gain,
    proj_weight,
    proj_bias,
    upstream,
):
    dp, tm = lax.axis_size("dp"), lax.axis_size("tm")
    recs_local, length, channels = features.shape
    pairs, frames_total, depth = upstream.shape
    frames = frames_total // tm
    if not (dp == 4 and tm == 8 and recs_local == 1 and frames % 128 == 0 and HEADS * depth % 128 == 0 and pairs * tm == HEADS):
        return generic_shards(
            features,
            conv_wide,
            conv_narrow,
            conv_bias,
            norm_gain,
            norm_bias,
            proj_gain,
            proj_weight,
            proj_bias,
            upstream,
        )
    width = HEADS * depth
    factor = 1.0 / math.sqrt(recs_local * dp * frames_total)
    sems = [pltpu.SemaphoreType.DMA((tm,))]
    signal = features.reshape(length, channels)
    frames_cut = (pairs, depth, frames)
    early = (1, 7)
    late = [k for k in range(tm) if k not in early]
    *cuts, first_rows = local(
        lambda *refs: first_cut_kernel(early, *refs),
        [upstream.transpose(0, 2, 1), signal],
        [(frames_cut, BF16, True)] * len(early) + [((8, channels), BF16, True)],
        "cut",
        scratch=[pltpu.SemaphoreType.DMA((len(early) + 1,))],
        raw=(0, 1),
    )
    cuts += local(
        lambda *refs: rest_cut_kernel(late, *refs),
        [upstream.transpose(0, 2, 1)],
        [(frames_cut, BF16, False)] * len(late),
        "rest_cut",
        scratch=[pltpu.VMEM((len(late), *frames_cut), BF16)] + [pltpu.SemaphoreType.DMA((len(late),))] * 2,
        raw=(0,),
        raw_out=range(len(late)),
    )
    cuts = {k: cut.reshape(pairs * depth, frames) for k, cut in zip([*early, *late], cuts)}
    heads_in = {0: cuts[0]}
    for k in ORDER[1:]:
        heads_in[k] = swap(cuts[k], 0, 0, k // 2, k % 2)
    halo = passed_along(first_rows, "tm", -1)
    wide_rows = 2 * frames
    spread = pltpu.VMEM((channels // 128, length, 128), F32)
    gain = proj_gain.reshape(1, channels)
    forward_in = [
        signal,
        halo,
        conv_bias,
        norm_gain,
        norm_bias,
        conv_wide,
        conv_narrow,
        gain,
        proj_bias.reshape(width // 128, 128),
        proj_weight,
    ]
    forward_out = [
        ((width, frames), BF16, False),
        ((3 * channels, wide_rows), BF16, False),
        ((2 * channels, frames), BF16, False),
        ((wide_rows, channels), F32, False),
        ((wide_rows, channels), F32, False),
        ((wide_rows, 128), F32, False),
        ((frames, channels), F32, False),
        ((frames, channels), F32, False),
        ((frames, 128), F32, False),
        ((frames, channels), F32, False),
        ((frames, 128), F32, False),
    ]
    proj_t, *stored = local(
        forward_kernel,
        forward_in,
        forward_out,
        "forward",
        limit=40,
        scratch=[pltpu.VMEM(x.shape, x.dtype) for x in forward_in]
        + [pltpu.VMEM(shape, dtype) for shape, dtype, _ in forward_out]
        + [
            pltpu.SemaphoreType.DMA((len(forward_in),)),
            pltpu.SemaphoreType.DMA((len(forward_out),)),
            spread,
            pltpu.VMEM((wide_rows, 3 * channels), BF16),
        ],
        raw=range(len(forward_in)),
        raw_out=range(len(forward_out)),
    )
    proj_t, heads_in[1] = lax.optimization_barrier((proj_t, heads_in[1]))
    heads = lax.all_to_all(
        proj_t.reshape(tm, pairs * depth, frames), "tm", split_axis=0, concat_axis=0, tiled=True
    )
    outer, inner = dp // 2, tm
    part_rows = 5 * channels // (dp * tm)
    part = ((outer, inner, part_rows, channels), BF16, True)
    patch_t, act_t, normed_w, slope_w, inv_w, normed_n, slope_n, inv_n, unit, row_inv = stored
    inputs = [
        proj_weight,
        *[heads_in[k] for k in ORDER],
        gain,
        unit,
        row_inv,
        normed_n,
        slope_n,
        inv_n,
        conv_narrow,
        normed_w,
        slope_w,
        inv_w,
        patch_t,
        act_t,
    ]
    lefts = [
        pltpu.VMEM((x.shape[0] // (2 * outer), x.shape[1]), BF16)
        for x in (patch_t, act_t)
        for _ in range(outer)
    ]
    held = [pltpu.VMEM(x.shape, x.dtype) for x in inputs[:1] + inputs[tm + 1 : -2]]
    held = held[:-3] + lefts[outer:] + held[-3:] + lefts[:outer]
    grad_buf = pltpu.VMEM((width, frames), BF16)
    send, grad_conv, grad_low = local(
        lambda *refs: backward_kernel(factor, *refs),
        inputs,
        [part, ((wide_rows, channels), BF16, True), ((frames, channels), BF16, True)],
        "backward",
        limit=24,
        scratch=held + [grad_buf, pltpu.SemaphoreType.DMA((len(held) + tm + 1,))],
        raw=range(len(inputs)),
        free=range(1, tm + 1),
    )
    received = swap(send, 0, 1, 0, 0)
    held = lefts + [pltpu.VMEM((channels, channels), BF16)]
    keep, tail = local(
        lambda *refs: own_grad_kernel(factor, *refs),
        [patch_t, act_t, conv_wide, grad_conv, grad_low],
        [part, ((8, channels), F32, True)],
        "own_grad",
        scratch=held + [pltpu.SemaphoreType.DMA((len(held),))],
        raw=(0, 1, 2),
    )
    plane = ((tm // 2, part_rows, channels), BF16, True)
    own, *outgoing = local(first_sum_kernel, [keep, received], [plane] * 4, "first_sum")
    arrived = [swap(outgoing[k - 1], k // 2, 0, 0, k % 2) for k in (3, 2, 1)]
    tail, grad_conv, own = lax.optimization_barrier((tail, grad_conv, own))
    incoming = passed_along(tail, "tm", 1)
    feature_grad, first_rows = local(
        input_grad_kernel,
        [grad_conv, conv_wide],
        [((length, channels), BF16, False), ((8, channels), F32, True)],
        "input_grad",
        scratch=[spread],
    )
    piece = ((part_rows, channels), BF16, True)
    (attn_t,) = local(
        join_kernel,
        [heads.reshape(tm, pairs, depth, frames)],
        [((pairs, depth, frames_total), BF16, False)],
        "join",
        scratch=sems,
        raw_out=(0,),
    )
    attn_t, first_rows, incoming, own = lax.optimization_barrier((attn_t, first_rows, incoming, own))
    own, *outgoing = local(second_sum_kernel, [own, *arrived], [piece] * 4, "second_sum")
    arrived = [swap(outgoing[k - 1], 0, 0, k, 0) for k in (2, 1, 3)]
    own_wide = 3 * channels // (dp * tm)
    first_rows, own = lax.optimization_barrier((first_rows, own))
    (feature_grad,) = local(
        first_row_kernel,
        [incoming, first_rows, feature_grad],
        [((length, channels), BF16, False)],
        "first_row",
        scratch=[pltpu.VMEM((8, channels), BF16), pltpu.SemaphoreType.DMA((1,))],
        raw=(2,),
        raw_out=(0,),
        aliases={2: 0},
    )
    feature_grad, own = lax.optimization_barrier((feature_grad, own))
    wide, narrow = local(
        lambda *refs: last_sum_kernel(own_wide, *refs),
        [own, *arrived],
        [
            ((own_wide * channels // 128, 128), F32, False),
            (((part_rows - own_wide) * channels // 128, 128), F32, False),
        ],
        "last_sum",
    )
    return (
        attn_t.transpose(0, 2, 1),
        feature_grad.reshape(recs_local, length, channels),
        wide.reshape(-1),
        narrow.reshape(-1),
    )


def solution(mesh):
    in_specs = (
        P("dp", "tm", None),
        P(),
        P(),
        P(),
        P(),
        P(),
        P(),
        P(),
        P(),
        P(("dp", "tm"), None, None),
    )
    out_specs = (P(("dp", "tm"), None, None), P("dp", "tm", None), P(("dp", "tm")), P(("dp", "tm")))
    return jax.shard_map(shards, mesh=mesh, in_specs=in_specs, out_specs=out_specs, check_vma=False)
```

```python
import math

import jax
import jax.numpy as jnp
from jax import lax
from jax.experimental import pallas as pl
from jax.experimental.pallas import tpu as pltpu
from jax.sharding import PartitionSpec as P

HEADS = 16
HEAD_DIM = 120


EPSILON = 1e-05
SQRT_HALF = 0.7071067811865476
INV_ROOT_TAU = 0.3989422804014327


def passed_along(value, axis, steps):
    count = lax.axis_size(axis)
    leading, last = (max(0, -steps), min(count, count - steps))
    return lax.ppermute(value, axis, [(source, source + steps) for source in range(leading, last)])


def gelu_exact(values):
    return 0.5 * values * (1.0 + lax.erf(values * SQRT_HALF))


def gelu_slope(values):
    cumulative = 0.5 * (1.0 + lax.erf(values * SQRT_HALF))
    density = jnp.exp(-0.5 * values * values) * INV_ROOT_TAU
    return cumulative + values * density


def wide_patches(signal, first_next):
    recs_local, length, channels = signal.shape
    paired = signal.reshape(recs_local, length // 2, 2 * channels)
    following = jnp.concatenate([paired[:, 1:, :channels], first_next], axis=1)
    return jnp.concatenate([paired, following], axis=2)


def narrow_patches(signal):
    recs_local, length, channels = signal.shape
    return signal.reshape(recs_local, length // 2, 2 * channels)


def conv_forward(patches, weight, bias_conv, gain_row, bias_row):
    recs_local, out_rows, patch_width = patches.shape
    conv_out = jnp.dot(
        patches.reshape(recs_local * out_rows, patch_width),
        weight,
        preferred_element_type=jnp.float32,
    )
    conv_out = conv_out.reshape(recs_local, out_rows, weight.shape[1]) + bias_conv
    center = jnp.mean(conv_out, axis=2, keepdims=True)
    centered = conv_out - center
    inverse = lax.rsqrt(jnp.mean(centered * centered, axis=2, keepdims=True) + EPSILON)
    normed = centered * inverse
    preact = normed * gain_row + bias_row
    activated = gelu_exact(preact).astype(jnp.bfloat16)
    return (activated, (patches, normed, preact, inverse))


def conv_backward(grad_act, weight, gain_row, stored):
    patches, normed, preact, inverse = stored
    recs_local, out_rows, patch_width = patches.shape
    grad_normed = grad_act.astype(jnp.float32) * gelu_slope(preact) * gain_row
    avg_grad = jnp.mean(grad_normed, axis=2, keepdims=True)
    avg_cross = jnp.mean(grad_normed * normed, axis=2, keepdims=True)
    grad_conv = (inverse * (grad_normed - avg_grad - normed * avg_cross)).astype(jnp.bfloat16)
    flat_patches = patches.reshape(recs_local * out_rows, patch_width)
    flat_grad = grad_conv.reshape(recs_local * out_rows, weight.shape[1])
    weight_grad = lax.dot_general(
        flat_patches, flat_grad, (((0,), (0,)), ((), ())), preferred_element_type=jnp.float32
    )
    grad_patch = lax.dot_general(
        flat_grad, weight, (((1,), (1,)), ((), ())), preferred_element_type=jnp.float32
    )
    return (weight_grad, grad_patch.reshape(recs_local, out_rows, patch_width))


def wide_input_grad(grad_patch, channels):
    recs_local, out_rows, patch_width = grad_patch.shape
    tail = grad_patch[:, :, 2 * channels :]
    incoming = passed_along(tail[:, -1:], "tm", 1)
    shifted = jnp.concatenate([incoming, tail[:, :-1]], axis=1)
    first_half = grad_patch[:, :, :channels] + shifted
    combined = jnp.concatenate([first_half, grad_patch[:, :, channels : 2 * channels]], axis=2)
    return combined.reshape(recs_local, 2 * out_rows, channels).astype(jnp.bfloat16)


def narrow_input_grad(grad_patch, channels):
    recs_local, out_rows, patch_width = grad_patch.shape
    return grad_patch.reshape(recs_local, 2 * out_rows, channels).astype(jnp.bfloat16)


def share_grad(weight_grad, factor):
    flat = (weight_grad * factor).reshape(-1)
    result = lax.psum_scatter(flat, ("dp", "tm"), scatter_dimension=0, tiled=True)
    return result


def generic_shards(
    features,
    conv_wide,
    conv_narrow,
    conv_bias,
    norm_gain,
    norm_bias,
    proj_gain,
    proj_weight,
    proj_bias,
    upstream,
):
    recs_local, length, channels = features.shape
    tm_count = lax.axis_size("tm")
    frames_total = upstream.shape[1]
    frames_local = frames_total // tm_count
    factor = 1.0 / math.sqrt(recs_local * lax.axis_size("dp") * frames_total)
    grad_frames = lax.all_to_all(upstream, "tm", split_axis=1, concat_axis=0, tiled=True)
    first_next = passed_along(features[:, :1], "tm", -1)
    act_wide, stored_wide = conv_forward(
        wide_patches(features, first_next), conv_wide, conv_bias[0], norm_gain[0], norm_bias[0]
    )
    act_narrow, stored_narrow = conv_forward(
        narrow_patches(act_wide), conv_narrow, conv_bias[1], norm_gain[1], norm_bias[1]
    )
    widened = act_narrow.astype(jnp.float32)
    centered = widened - jnp.mean(widened, axis=2, keepdims=True)
    row_inverse = lax.rsqrt(jnp.mean(centered * centered, axis=2, keepdims=True) + EPSILON)
    unit_rows = centered * row_inverse
    normed_in = (unit_rows * proj_gain).astype(jnp.bfloat16)
    weight_heads = proj_weight.reshape(channels, HEADS, HEAD_DIM)
    projected = jnp.einsum(
        "rfc,chd->rhfd", normed_in, weight_heads, preferred_element_type=jnp.float32
    ) + proj_bias.reshape(HEADS, 1, HEAD_DIM)
    heads_local = projected.astype(jnp.bfloat16).reshape(recs_local * HEADS, frames_local, HEAD_DIM)
    attn_input = lax.all_to_all(heads_local, "tm", split_axis=0, concat_axis=1, tiled=True)
    grad_heads = grad_frames.reshape(recs_local, HEADS, frames_local, HEAD_DIM)
    grad_unit = (
        jnp.einsum("rhfd,chd->rfc", grad_heads, weight_heads, preferred_element_type=jnp.float32)
        * proj_gain
    )
    grad_last = (
        row_inverse
        * (
            grad_unit
            - jnp.mean(grad_unit, axis=2, keepdims=True)
            - unit_rows * jnp.mean(grad_unit * unit_rows, axis=2, keepdims=True)
        )
    ).astype(jnp.bfloat16)
    weight_narrow, patch_narrow = conv_backward(grad_last, conv_narrow, norm_gain[1], stored_narrow)
    grad_conv_narrow = share_grad(weight_narrow, factor)
    grad_first = narrow_input_grad(patch_narrow, channels)
    weight_wide, patch_wide = conv_backward(grad_first, conv_wide, norm_gain[0], stored_wide)
    grad_conv_wide = share_grad(weight_wide, factor)
    feature_grad = wide_input_grad(patch_wide, channels)
    return (attn_input, feature_grad, grad_conv_wide, grad_conv_narrow)


F32 = jnp.float32
ORDER = (0, 7, 6, 4, 3, 5, 2, 1)
BF16 = jnp.bfloat16
NT = (((1,), (1,)), ((), ()))


def dot(a, b):
    return jnp.dot(a, b, preferred_element_type=F32)


def dot_nt(a, b):
    return lax.dot_general(a, b, NT, preferred_element_type=F32)


def row_mean(values):
    return jnp.mean(values, axis=1, keepdims=True)


def normalized(values):
    centered = values - row_mean(values)
    inverse = lax.rsqrt(row_mean(centered * centered) + EPSILON)
    return centered * inverse, inverse


def gelu_parts(preact):
    cumulative = 0.5 * (1.0 + lax.erf(preact * SQRT_HALF))
    slope = cumulative + preact * (jnp.exp(-0.5 * preact * preact) * INV_ROOT_TAU)
    return preact * cumulative, slope


def local(kernel, operands, outs, name, limit=16, scratch=(), raw=(), raw_out=(), free=(), aliases=None, cost=1000):
    out_shape, out_specs = [], []
    for number, (shape, dtype, stays) in enumerate(outs):
        out_shape.append((pltpu.VMEM if stays else pltpu.HBM)(shape, dtype))
        out_specs.append(pl.BlockSpec(memory_space=pltpu.HBM if number in raw_out else pltpu.VMEM))
    held = [
        x if k in free else pltpu.with_memory_space_constraint(x, pltpu.HBM if k in raw else pltpu.VMEM)
        for k, x in enumerate(operands)
    ]
    return pl.pallas_call(
        kernel,
        out_shape=out_shape,
        in_specs=[
            pl.BlockSpec(memory_space=pl.ANY if k in free else pltpu.HBM if k in raw else pltpu.VMEM)
            for k in range(len(operands))
        ],
        out_specs=out_specs,
        scratch_shapes=list(scratch),
        input_output_aliases=aliases or {},
        compiler_params=pltpu.CompilerParams(vmem_limit_bytes=limit << 20),
        cost_estimate=pl.CostEstimate(flops=cost, bytes_accessed=0, transcendentals=0),
        name=name,
    )(*held)


def run_copies(pairs, sems):
    copies = [pltpu.make_async_copy(src, dst, sems.at[k]) for k, (src, dst) in enumerate(pairs)]
    for copy in copies:
        copy.start()
    for copy in copies:
        copy.wait()


def first_cut_kernel(flips, whole, signal, *refs):
    *parts, first_rows, sems = refs
    width = parts[0].shape[2]
    own = lax.axis_index("tm")
    starts = [pl.multiple_of((own ^ flip) * width, width) for flip in flips]
    pairs = [(whole.at[:, :, pl.ds(start, width)], part) for start, part in zip(starts, parts)]
    run_copies([*pairs, (signal.at[pl.ds(0, 8), :], first_rows)], sems)


def rest_cut_kernel(flips, whole, *refs):
    *parts, held, sems, out_sems = refs
    width = held.shape[3]
    own = lax.axis_index("tm")
    reads, writes = [], []
    for k, flip in enumerate(flips):
        start = pl.multiple_of((own ^ flip) * width, width)
        reads.append(pltpu.make_async_copy(whole.at[:, :, pl.ds(start, width)], held.at[k], sems.at[k]))
        writes.append(pltpu.make_async_copy(held.at[k], parts[k], out_sems.at[k]))
    for read in reads:
        read.start()
    for read, write in zip(reads, writes):
        read.wait()
        write.start()
    for write in writes:
        write.wait()


def join_kernel(parts, whole, sems):
    width = parts.shape[3]
    run_copies([(parts.at[k], whole.at[:, :, pl.ds(k * width, width)]) for k in range(parts.shape[0])], sems)


class Loads:
    def __init__(self, sources, held, sems):
        self.pairs = [
            (pltpu.make_async_copy(src, buf, sems.at[k]), buf) for k, (src, buf) in enumerate(zip(sources, held))
        ]
        for read, _ in self.pairs:
            read.start()

    def take(self, count):
        taken, self.pairs = self.pairs[:count], self.pairs[count:]
        for read, _ in taken:
            read.wait()
        return [buf for _, buf in taken]


def spread_rows(spread, first, count):
    lanes = [spread[lane, pl.ds(first, count, stride=4), :] for lane in range(spread.shape[0])]
    return jnp.concatenate(lanes, axis=1)


def put_rows(spread, first, value):
    for lane in range(spread.shape[0]):
        spread[lane, pl.ds(first, value.shape[0], stride=4), :] = value[:, lane * 128 : (lane + 1) * 128]


def forward_kernel(*refs):
    sources, outs, rest = refs[:10], refs[10:21], refs[21:]
    *held, sems, out_sems, spread, patches = rest
    held, bufs = held[:10], held[10:]
    writes = []

    def put(number):
        write = pltpu.make_async_copy(bufs[number], outs[number], out_sems.at[number])
        write.start()
        writes.append(write)

    (
        proj_t,
        patch_t,
        act_t,
        normed_w,
        slope_w,
        inv_w,
        normed_n,
        slope_n,
        inv_n,
        unit_out,
        row_inv,
    ) = bufs
    loads = Loads(sources, held, sems)
    feat, halo, conv_bias, norm_gain, norm_bias = loads.take(5)
    frames = feat.shape[0] // 4
    channels = feat.shape[1]
    for lane in range(channels // 128):
        spread[lane] = feat[:, lane * 128 : (lane + 1) * 128].astype(F32)
    rows = [spread_rows(spread, j, frames) for j in range(4)]
    following = pltpu.roll(rows[0], frames - 1, axis=0)
    at_end = lax.broadcasted_iota(jnp.int32, (frames, 1), 0) == frames - 1
    rows.append(jnp.where(at_end, halo[0:1, :].astype(F32), following))
    rows = [row.astype(BF16) for row in rows]
    for parity in range(2):
        for tap in range(3):
            piece = rows[2 * parity + tap]
            patches[parity * frames : (parity + 1) * frames, tap * channels : (tap + 1) * channels] = piece
            patch_t[tap * channels : (tap + 1) * channels, parity * frames : (parity + 1) * frames] = piece.T
    put(1)
    (conv_wide,) = loads.take(1)
    conv = dot(patches[...], conv_wide[...]) + conv_bias[0:1, :]
    normed, inverse = normalized(conv)
    normed_w[...] = normed
    inv_w[...] = jnp.broadcast_to(inverse, inv_w.shape)
    put(3)
    put(5)
    act, slope = gelu_parts(normed * norm_gain[0:1, :] + norm_bias[0:1, :])
    slope_w[...] = slope * norm_gain[0:1, :]
    put(4)
    act = act.astype(BF16)
    even, odd = act[:frames], act[frames:]
    act_t[0:channels, :] = even.T
    act_t[channels:, :] = odd.T
    put(2)
    (conv_narrow,) = loads.take(1)
    conv = dot(even, conv_narrow[0:channels, :]) + dot(odd, conv_narrow[channels:, :]) + conv_bias[1:2, :]
    normed, inverse = normalized(conv)
    normed_n[...] = normed
    inv_n[...] = jnp.broadcast_to(inverse, inv_n.shape)
    put(6)
    put(8)
    act, slope = gelu_parts(normed * norm_gain[1:2, :] + norm_bias[1:2, :])
    slope_n[...] = slope * norm_gain[1:2, :]
    put(7)
    unit, inverse = normalized(act.astype(BF16).astype(F32))
    unit_out[...] = unit
    row_inv[...] = jnp.broadcast_to(inverse, row_inv.shape)
    put(9)
    put(10)
    proj_gain, proj_bias, proj_weight = loads.take(3)
    normed_in = (unit * proj_gain[...]).astype(BF16)
    bias = jnp.concatenate([proj_bias[k : k + 1, :] for k in range(proj_bias.shape[0])], axis=1)
    projected = dot(normed_in, proj_weight[...]) + bias
    proj_t[...] = projected.astype(BF16).T
    put(0)
    for write in writes:
        write.wait()


def owned_rows(left, owner, outer):
    part = left.shape[0] // (2 * outer)
    return [left.at[pl.ds(pl.multiple_of((2 * block + owner) * part, part), part), :] for block in range(outer)]


def weight_grad(loads, grad, factor, target, low):
    outer, inner, height = target.shape[0], target.shape[1], target.shape[2]
    for block, left in enumerate(loads.take(outer)):
        value = (dot(left[...], grad) * factor).astype(BF16)
        each = left.shape[0] // inner
        row = height - each if low else 0
        for k in range(inner):
            target[block, k, row : row + each, :] = value[k * each : (k + 1) * each]


def backward_kernel(factor, *refs):
    tm = lax.axis_size("tm")
    count = 13 + tm
    sources, (send, grad_conv, grad_low), rest = refs[:count], refs[count : count + 3], refs[count + 3 :]
    *held, grad_t, sems = rest
    outer = send.shape[0]
    own = lax.axis_index("tm")
    rows = sources[1].shape[0]
    places = [grad_t.at[pl.ds(pl.multiple_of((own ^ k) * rows, rows), rows), :] for k in ORDER]
    other = 1 - lax.axis_index("dp") % 2
    wide_left, low_left = (owned_rows(left, other, outer) for left in sources[-2:])
    cut = held[0].shape[1] * 8 // 15
    halves = [pl.ds(0, cut), pl.ds(cut, held[0].shape[1] - cut)]
    loads = Loads([*sources[1 : 1 + tm], *(sources[0].at[:, at] for at in halves), *sources[1 + tm : -5], *low_left, *sources[-5:-2], *wide_left], [*places, *(held[0].at[:, at] for at in halves), *held[1:]], sems)
    loads.take(tm)
    product = dot(loads.take(1)[0][...], grad_t[0:cut, :])
    right, proj_gain = loads.take(2)
    grad_unit = (product + dot(right[...], grad_t[cut:, :])).T * proj_gain[...]
    unit_in, row_inv = loads.take(2)
    frames, channels = unit_in.shape
    unit = unit_in[...]
    grad_last = row_inv[:, 0:1] * (grad_unit - row_mean(grad_unit) - unit * row_mean(grad_unit * unit))
    normed_n, slope_n, inv_n, conv_narrow = loads.take(4)
    grad_normed = grad_last.astype(BF16).astype(F32) * slope_n[...]
    normed = normed_n[...]
    grad_narrow = (
        inv_n[:, 0:1] * (grad_normed - row_mean(grad_normed) - normed * row_mean(grad_normed * normed))
    ).astype(BF16)
    grad_low[...] = grad_narrow
    weight_grad(loads, grad_narrow, factor, send, True)
    normed_w, slope_w, inv_w = loads.take(3)
    for parity in range(2):
        at = pl.ds(parity * frames, frames)
        grad_first = dot_nt(grad_narrow, conv_narrow[parity * channels : (parity + 1) * channels, :]).astype(BF16)
        grad_normed = grad_first.astype(F32) * slope_w[at, :]
        normed = normed_w[at, :]
        grad_conv[at, :] = (
            inv_w[at, 0:1] * (grad_normed - row_mean(grad_normed) - normed * row_mean(grad_normed * normed))
        ).astype(BF16)
    weight_grad(loads, grad_conv[...], factor, send, False)


def own_grad_kernel(factor, patch_t, act_t, conv_wide, grad_conv, grad_low, keep, tail, *rest):
    held, sems = rest[:-1], rest[-1]
    outer = keep.shape[0]
    core = lax.axis_index("dp") % 2
    lefts = [rows for left in (patch_t, act_t) for rows in owned_rows(left, core, outer)]
    last_tap = held[-1].shape[0]
    loads = Loads([*lefts, conv_wide.at[pl.ds(2 * last_tap, last_tap), :]], held, sems)
    grad_wide = grad_conv[...]
    weight_grad(loads, grad_wide, factor, keep, False)
    weight_grad(loads, grad_low[...], factor, keep, True)
    (tap,) = loads.take(1)
    tail[...] = dot_nt(grad_wide[grad_wide.shape[0] - 8 :, :], tap[...])


def input_grad_kernel(grad_conv, conv_wide, out, first_rows, spread):
    frames = grad_conv.shape[0] // 2
    channels = grad_conv.shape[1]
    even, odd = grad_conv[:frames, :], grad_conv[frames:, :]
    taps = [conv_wide[tap * channels : (tap + 1) * channels, :] for tap in range(3)]
    shifted = pltpu.roll(dot_nt(odd, taps[2]), 1, axis=0)
    at_start = lax.broadcasted_iota(jnp.int32, (frames, 1), 0) == 0
    shifted = jnp.where(at_start, 0.0, shifted)
    put_rows(spread, 0, dot_nt(even, taps[0]) + shifted)
    put_rows(spread, 1, dot_nt(even, taps[1]))
    put_rows(spread, 2, dot_nt(even, taps[2]) + dot_nt(odd, taps[0]))
    put_rows(spread, 3, dot_nt(odd, taps[1]))
    for lane in range(channels // 128):
        out[:, lane * 128 : (lane + 1) * 128] = spread[lane].astype(BF16)
        first_rows[:, lane * 128 : (lane + 1) * 128] = spread[lane, 0:8, :]


def first_sum_kernel(keep, received, *outs):
    y = lax.axis_index("dp") // 2
    x = lax.axis_index("tm") % 2
    inner = keep.shape[1] // 2
    for flip, out in enumerate(outs):
        block = y ^ (flip // 2)
        lane = x ^ (flip % 2)
        for z in range(inner):
            at = 2 * z + lane
            out[z] = (keep[block, at].astype(F32) + received[block, at].astype(F32)).astype(BF16)


def second_sum_kernel(a, b, c, d, *outs):
    z = lax.axis_index("tm") // 2
    for flip, out in enumerate(outs):
        at = z ^ flip
        total = (a[at].astype(F32) + b[at].astype(F32)) + (c[at].astype(F32) + d[at].astype(F32))
        out[...] = total.astype(BF16)


def first_row_kernel(incoming, first_rows, grad_in, grad_out, rows_buf, sem):
    at_start = lax.broadcasted_iota(jnp.int32, (8, 1), 0) == 0
    rows_buf[...] = (first_rows[...] + jnp.where(at_start, incoming[7:8, :], 0.0)).astype(BF16)
    run_copies([(rows_buf, grad_out.at[pl.ds(0, 8), :])], sem)


def last_sum_kernel(wide_rows, a, b, c, d, wide, narrow):
    total = (a[...].astype(F32) + b[...].astype(F32)) + (c[...].astype(F32) + d[...].astype(F32))
    rows, channels = total.shape
    pieces = channels // 128
    for p in range(pieces):
        lanes = total[:, p * 128 : (p + 1) * 128]
        wide[pl.ds(p, wide_rows, stride=pieces), :] = lanes[:wide_rows]
        narrow[pl.ds(p, rows - wide_rows, stride=pieces), :] = lanes[wide_rows:]


def flipped(dy, dc, dz, dx):
    dp, tm = lax.axis_size("dp"), lax.axis_size("tm")
    change_dp, change_tm = 2 * dy + dc, 2 * dz + dx
    return [
        (p * tm + t, (p ^ change_dp) * tm + (t ^ change_tm)) for p in range(dp) for t in range(tm)
    ]


def swap(value, dy, dc, dz, dx):
    return lax.ppermute(value, ("dp", "tm"), flipped(dy, dc, dz, dx))


def shards(
    features,
    conv_wide,
    conv_narrow,
    conv_bias,
    norm_gain,
    norm_bias,
    proj_gain,
    proj_weight,
    proj_bias,
    upstream,
):
    dp, tm = lax.axis_size("dp"), lax.axis_size("tm")
    recs_local, length, channels = features.shape
    pairs, frames_total, depth = upstream.shape
    frames = frames_total // tm
    if not (dp == 4 and tm == 8 and recs_local == 1 and frames % 128 == 0 and HEADS * depth % 128 == 0 and pairs * tm == HEADS):
        return generic_shards(
            features,
            conv_wide,
            conv_narrow,
            conv_bias,
            norm_gain,
            norm_bias,
            proj_gain,
            proj_weight,
            proj_bias,
            upstream,
        )
    width = HEADS * depth
    factor = 1.0 / math.sqrt(recs_local * dp * frames_total)
    sems = [pltpu.SemaphoreType.DMA((tm,))]
    signal = features.reshape(length, channels)
    frames_cut = (pairs, depth, frames)
    early = (1, 7)
    late = [k for k in range(tm) if k not in early]
    *cuts, first_rows = local(
        lambda *refs: first_cut_kernel(early, *refs),
        [upstream.transpose(0, 2, 1), signal],
        [(frames_cut, BF16, True)] * len(early) + [((8, channels), BF16, True)],
        "cut",
        scratch=[pltpu.SemaphoreType.DMA((len(early) + 1,))],
        raw=(0, 1),
    )
    cuts += local(
        lambda *refs: rest_cut_kernel(late, *refs),
        [upstream.transpose(0, 2, 1)],
        [(frames_cut, BF16, False)] * len(late),
        "rest_cut",
        scratch=[pltpu.VMEM((len(late), *frames_cut), BF16)] + [pltpu.SemaphoreType.DMA((len(late),))] * 2,
        raw=(0,),
        raw_out=range(len(late)),
    )
    cuts = {k: cut.reshape(pairs * depth, frames) for k, cut in zip([*early, *late], cuts)}
    heads_in = {0: cuts[0]}
    for k in ORDER[1:]:
        heads_in[k] = swap(cuts[k], 0, 0, k // 2, k % 2)
    halo = passed_along(first_rows, "tm", -1)
    wide_rows = 2 * frames
    spread = pltpu.VMEM((channels // 128, length, 128), F32)
    gain = proj_gain.reshape(1, channels)
    forward_in = [
        signal,
        halo,
        conv_bias,
        norm_gain,
        norm_bias,
        conv_wide,
        conv_narrow,
        gain,
        proj_bias.reshape(width // 128, 128),
        proj_weight,
    ]
    forward_out = [
        ((width, frames), BF16, False),
        ((3 * channels, wide_rows), BF16, False),
        ((2 * channels, frames), BF16, False),
        ((wide_rows, channels), F32, False),
        ((wide_rows, channels), F32, False),
        ((wide_rows, 128), F32, False),
        ((frames, channels), F32, False),
        ((frames, channels), F32, False),
        ((frames, 128), F32, False),
        ((frames, channels), F32, False),
        ((frames, 128), F32, False),
    ]
    proj_t, *stored = local(
        forward_kernel,
        forward_in,
        forward_out,
        "forward",
        limit=40,
        scratch=[pltpu.VMEM(x.shape, x.dtype) for x in forward_in]
        + [pltpu.VMEM(shape, dtype) for shape, dtype, _ in forward_out]
        + [
            pltpu.SemaphoreType.DMA((len(forward_in),)),
            pltpu.SemaphoreType.DMA((len(forward_out),)),
            spread,
            pltpu.VMEM((wide_rows, 3 * channels), BF16),
        ],
        raw=range(len(forward_in)),
        raw_out=range(len(forward_out)),
    )
    proj_t, heads_in[1] = lax.optimization_barrier((proj_t, heads_in[1]))
    heads = lax.all_to_all(
        proj_t.reshape(tm, pairs * depth, frames), "tm", split_axis=0, concat_axis=0, tiled=True
    )
    outer, inner = dp // 2, tm
    part_rows = 5 * channels // (dp * tm)
    part = ((outer, inner, part_rows, channels), BF16, True)
    patch_t, act_t, normed_w, slope_w, inv_w, normed_n, slope_n, inv_n, unit, row_inv = stored
    inputs = [
        proj_weight,
        *[heads_in[k] for k in ORDER],
        gain,
        unit,
        row_inv,
        normed_n,
        slope_n,
        inv_n,
        conv_narrow,
        normed_w,
        slope_w,
        inv_w,
        patch_t,
        act_t,
    ]
    lefts = [
        pltpu.VMEM((x.shape[0] // (2 * outer), x.shape[1]), BF16)
        for x in (patch_t, act_t)
        for _ in range(outer)
    ]
    held = [pltpu.VMEM(x.shape, x.dtype) for x in inputs[:1] + inputs[tm + 1 : -2]]
    held = held[:-3] + lefts[outer:] + held[-3:] + lefts[:outer]
    grad_buf = pltpu.VMEM((width, frames), BF16)
    send, grad_conv, grad_low = local(
        lambda *refs: backward_kernel(factor, *refs),
        inputs,
        [part, ((wide_rows, channels), BF16, True), ((frames, channels), BF16, True)],
        "backward",
        limit=24,
        scratch=held + [grad_buf, pltpu.SemaphoreType.DMA((len(held) + tm + 1,))],
        raw=range(len(inputs)),
        free=range(1, tm + 1),
    )
    received = swap(send, 0, 1, 0, 0)
    held = lefts + [pltpu.VMEM((channels, channels), BF16)]
    keep, tail = local(
        lambda *refs: own_grad_kernel(factor, *refs),
        [patch_t, act_t, conv_wide, grad_conv, grad_low],
        [part, ((8, channels), F32, True)],
        "own_grad",
        scratch=held + [pltpu.SemaphoreType.DMA((len(held),))],
        raw=(0, 1, 2),
    )
    plane = ((tm // 2, part_rows, channels), BF16, True)
    own, *outgoing = local(first_sum_kernel, [keep, received], [plane] * 4, "first_sum")
    arrived = [swap(outgoing[k - 1], k // 2, 0, 0, k % 2) for k in (3, 2, 1)]
    tail, grad_conv, own = lax.optimization_barrier((tail, grad_conv, own))
    incoming = passed_along(tail, "tm", 1)
    feature_grad, first_rows = local(
        input_grad_kernel,
        [grad_conv, conv_wide],
        [((length, channels), BF16, False), ((8, channels), F32, True)],
        "input_grad",
        scratch=[spread],
    )
    piece = ((part_rows, channels), BF16, True)
    (attn_t,) = local(
        join_kernel,
        [heads.reshape(tm, pairs, depth, frames)],
        [((pairs, depth, frames_total), BF16, False)],
        "join",
        scratch=sems,
        raw_out=(0,),
    )
    attn_t, first_rows, own = lax.optimization_barrier((attn_t, first_rows, own))
    own, *outgoing = local(second_sum_kernel, [own, *arrived], [piece] * 4, "second_sum")
    arrived = [swap(outgoing[k - 1], 0, 0, k, 0) for k in (2, 1, 3)]
    own_wide = 3 * channels // (dp * tm)
    first_rows, own = lax.optimization_barrier((first_rows, own))
    (feature_grad,) = local(
        first_row_kernel,
        [incoming, first_rows, feature_grad],
        [((length, channels), BF16, False)],
        "first_row",
        scratch=[pltpu.VMEM((8, channels), BF16), pltpu.SemaphoreType.DMA((1,))],
        raw=(2,),
        raw_out=(0,),
        aliases={2: 0},
    )
    feature_grad, own = lax.optimization_barrier((feature_grad, own))
    wide, narrow = local(
        lambda *refs: last_sum_kernel(own_wide, *refs),
        [own, *arrived],
        [
            ((own_wide * channels // 128, 128), F32, False),
            (((part_rows - own_wide) * channels // 128, 128), F32, False),
        ],
        "last_sum",
    )
    return (
        attn_t.transpose(0, 2, 1),
        feature_grad.reshape(recs_local, length, channels),
        wide.reshape(-1),
        narrow.reshape(-1),
    )


def solution(mesh):
    in_specs = (
        P("dp", "tm", None),
        P(),
        P(),
        P(),
        P(),
        P(),
        P(),
        P(),
        P(),
        P(("dp", "tm"), None, None),
    )
    out_specs = (P(("dp", "tm"), None, None), P("dp", "tm", None), P(("dp", "tm")), P(("dp", "tm")))
    return jax.shard_map(shards, mesh=mesh, in_specs=in_specs, out_specs=out_specs, check_vma=False)
```
